512 devices in a mesh: obs: 16 (over y, x), space: 32 (over z, core).
Axes of the slice: x: 4, y: 4, z: 16, core: 2. Of those that a mesh axis runs over, the one named last changes fastest.
Arguments:
- probes: float32 [32, 4, 512, 256], P(None, None, 'space'), may hold values from -6 to 6
- wind: float32 [16, 2, 2, 4, 512, 256], P('obs', None, None, None, 'space'), may hold values from -0.6 to 0.6
- station_cell: int32 [16, 8192], P('obs', 'space'), may hold values from 0 to 16383
- obs_count: int32 [16, 32], P('obs', 'space'), may hold values from 1 to 256, as said below
- obs_weight: float32 [16, 8192], P('obs', 'space'), may hold values from 0.5 to 4
Outputs:
- basis: float32 [32, 4, 512, 256], P('obs', None, 'space')
- core: float32 [32, 32], replicated
The draws below stay inside these ranges and needn't reach their ends.
Inputs may be any that keep to these rules, and one draw needn't show every extreme that they name: `obs_count`: the live slots of a tile in a window are its first ones; some tile of some window has all 256 live.
All inputs are finite; a program needn't handle non-finite values.
Results may differ from the reference program's by a relative error of at most 0.0003.
Values sent between devices are 32-bit elements; how exact they have to be, the bound alone decides.
No kernel may reach another device: no remote copies, remote signals or barrier semaphores. Data moves between devices by JAX's collectives and lax.ppermute only.
A program may use at most 64 MiB of HBM per device.

```python
import math
import jax
import jax.numpy as jnp
from jax import lax

RX = 16
NY = 256
LEV = 4
PROBES = 32
STEPS = 2
SLOTS = 256
NX = 512
GROUPS = 16
TILES = 32
N_SPACE = 32


def draw_obs_count(key, part):
    first_key = jax.random.fold_in(key, 11)
    second_key = jax.random.fold_in(key, 23)
    raw = jax.random.randint(first_key, (GROUPS, TILES), 1, SLOTS + 1)
    counts = jnp.maximum(1, raw * raw // SLOTS).reshape(-1)
    spot = jax.random.randint(second_key, (), 0, GROUPS * TILES)
    counts = counts.at[spot].set(SLOTS)
    return counts.reshape(GROUPS, TILES).astype(jnp.int32)


def plant(values, key, smallest, top_value):
    dims = values.shape
    spot = [jax.random.randint(jax.random.fold_in(key, axis), (), 0, dims[axis]) for axis in range(len(dims))]
    values = values.at[tuple(spot)].set(smallest)
    longest = dims.index(max(dims))
    spot[longest] = (spot[longest] + 1) % dims[longest]
    return values.at[tuple(spot)].set(top_value)


def block_scale(own_key, dims, shards, least, top_value):
    factor_of = 1.0
    for position, blocks in shards:
        draws = jax.random.uniform(jax.random.fold_in(jax.random.fold_in(own_key, 6), position), (blocks,), jnp.float32, least / len(shards), top_value / len(shards))
        factor_of = factor_of * jnp.repeat(jnp.exp(draws), dims[position] // blocks).reshape((-1,) + (1,) * (len(dims) - 1 - position))
    return factor_of


def centred(key, dims, deviation, reach, cuts=(), held_as=jnp.bfloat16):
    values = jax.random.normal(key, dims, jnp.float32) * deviation
    if len(cuts) > 0:
        values = block_scale(key, dims, cuts, -0.22, 0.18) * values
    return jnp.clip(values, min=-reach, max=reach).astype(held_as)


def setup_inputs(seed: int = 0) -> dict:
    streams_of = jax.random.split(jax.random.key(seed), 6)
    probes = centred(streams_of[0], (PROBES, LEV, NX, NY), 1.0, 6.0, ((2, 32),), jnp.float32)
    wind = jnp.clip(jax.random.uniform(streams_of[1], (GROUPS, STEPS, 2, LEV, NX, NY), jnp.float32, -0.6, 0.6) * block_scale(streams_of[1], (GROUPS, STEPS, 2, LEV, NX, NY), ((0, 16), (4, 32)), -0.4, 0.0), -0.6, 0.6)
    station_cell = plant(jax.random.randint(streams_of[2], (GROUPS, TILES * SLOTS), 0, LEV * RX * NY), jax.random.fold_in(streams_of[2], 1), 0, (LEV * RX * NY) - 1).astype(jnp.int32)
    obs_count = draw_obs_count(jax.random.fold_in(streams_of[5], 71), 0)
    obs_weight = jnp.clip(jnp.exp(math.log(4.0) - 2.0794415 * jax.random.uniform(streams_of[4], (GROUPS, TILES * SLOTS), jnp.float32) ** block_scale(streams_of[4], (GROUPS, TILES * SLOTS), ((0, 16), (1, 32)), -0.2, 0.2)), 0.5, 4.0)
    return {"probes": probes, "wind": wind, "station_cell": station_cell, "obs_count": obs_count, "obs_weight": obs_weight}


def pad_rows(field):
    return jnp.pad(field, [(0, 0)] * (field.ndim - 2) + [(1, 1), (0, 0)])

def smooth_terms(centre, upper, lower):
    yplus = jnp.pad(centre, [(0, 0), (0, 0), (0, 0), (0, 1)])[:, :, :, 1:]
    yminus = jnp.pad(centre, [(0, 0), (0, 0), (0, 0), (1, 0)])[:, :, :, :-1]
    zplus = jnp.pad(centre, [(0, 0), (0, 1), (0, 0), (0, 0)])[:, 1:]
    zminus = jnp.pad(centre, [(0, 0), (1, 0), (0, 0), (0, 0)])[:, :-1]
    return (centre + 0.15 * (upper + lower + yplus + yminus - 4.0 * centre) + 0.1 * (zplus + zminus - 2.0 * centre), yplus, yminus)

def forward_advance(extended, wind_x, wind_y):
    centre = extended[:, :, 1:-1]
    upper = extended[:, :, 2:]
    lower = extended[:, :, :-2]
    result, yplus, yminus = smooth_terms(centre, upper, lower)
    return result - 0.5 * (wind_x * (upper - lower) + wind_y * (yplus - yminus))

def adjoint_advance(extended, wind_x_ext, wind_y):
    centre = extended[:, :, 1:-1]
    upper = extended[:, :, 2:]
    lower = extended[:, :, :-2]
    result, yplus, yminus = smooth_terms(centre, upper, lower)
    carried = wind_x_ext * extended
    across = wind_y * centre
    aplus = jnp.pad(across, [(0, 0), (0, 0), (0, 0), (0, 1)])[:, :, :, 1:]
    aminus = jnp.pad(across, [(0, 0), (0, 0), (0, 0), (1, 0)])[:, :, :, :-1]
    return result + 0.5 * (carried[:, :, 2:] - carried[:, :, :-2] + (aplus - aminus))

def reference(probes, wind, station_cell, obs_count, obs_weight):
    slot_ids = jnp.arange(N_SPACE * SLOTS, dtype=jnp.int32)
    tile_ids = (slot_ids // SLOTS).astype(jnp.int32)
    slot_in = (slot_ids % SLOTS).astype(jnp.int32)

    def one_group(total, inputs):
        wind_g, cells_g, count_g, weight_g = inputs
        field = probes
        for step in range(STEPS):
            field = forward_advance(pad_rows(field), wind_g[step, 0], wind_g[step, 1])
        level = cells_g // (RX * NY)
        rest = cells_g % (RX * NY)
        row_glob = tile_ids * RX + rest // NY
        column = rest % NY
        flat_index = ((level * NX + row_glob) * NY + column).astype(jnp.int32)
        live = (slot_in < count_g[tile_ids]).astype(probes.dtype)
        flat = field.reshape(PROBES, -1)
        sampled = flat[:, flat_index]
        weighted = sampled * (weight_g * live)[None, :]
        back = jnp.zeros_like(flat).at[:, flat_index].add(weighted).reshape(probes.shape)
        for step in reversed(range(STEPS)):
            back = adjoint_advance(pad_rows(back), pad_rows(wind_g[step, 0]), wind_g[step, 1])
        return (total + back, None)
    total, _ = lax.scan(one_group, jnp.zeros_like(probes), (wind, station_cell, obs_count, obs_weight))
    sketch = total.reshape(PROBES, -1)
    omega = probes.reshape(PROBES, -1)
    gram = jnp.dot(sketch, sketch.T, precision=lax.Precision.HIGHEST)
    core = jnp.dot(omega, sketch.T, precision=lax.Precision.HIGHEST) / (GROUPS * N_SPACE * SLOTS)
    lower = jnp.linalg.cholesky(gram)
    basis = jax.scipy.linalg.solve_triangular(lower, sketch, lower=True) * (LEV * NX * NY) ** 0.5
    return (basis.reshape(probes.shape), core)
```

```python
import math

import jax
import jax.numpy as jnp
from jax import lax
from jax.experimental import pallas as pl
from jax.experimental.pallas import tpu as pltpu
from jax.sharding import PartitionSpec as P

F32 = jnp.float32
HIGH = lax.Precision.HIGHEST
VM = pl.BlockSpec(memory_space=pltpu.VMEM)
SM = pl.BlockSpec(memory_space=pltpu.SMEM)
NT = (((1,), (1,)), ((), ()))

NP, LV, RX, NY = 32, 4, 16, 256
HALO = 4
ROWS = RX + 2 * HALO
LANES = 128
BLK = LV * NP
LINE = 2 * BLK
STRIDE = LV * RX * 2
AUX = HALO * LINE
SIDE = 56
MSG = AUX + 2 * SIDE


def iota(shape, dim):
    return lax.broadcasted_iota(jnp.int32, shape, dim)


def live_weights(weight_ref, count_ref):
    w = weight_ref[...]
    return jnp.where(iota(w.shape, 1) < count_ref[0, 0], w, 0.0)


def arrived(probes, x, h, l):
    first = ((l * 2 + x // 8) * 2 + h) * 8 + x % 8
    return probes[pl.ds(first, NP, stride=STRIDE), :]


def pack_kernel(probes, wind, cells, weight, count, up, down):
    cell_row = cells[...].astype(F32)
    live = live_weights(weight, count)
    for out, first in ((up, RX - HALO), (down, 0)):
        for xh in range(HALO):
            for h in range(2):
                for l in range(LV):
                    out[pl.ds(((xh * 2 + h) * LV + l) * NP, NP), :] = arrived(
                        probes, first + xh, h, l
                    )
        wfirst = RX - 3 if first else 0
        for h in range(2):
            at, cols = AUX + h * SIDE, pl.ds(h * LANES, LANES)
            for i in range(16):
                out[pl.ds(at + 3 * i, 3), :] = wind[pl.ds(i * RX + wfirst, 3), cols]
            out[pl.ds(at + 48, 1), :] = cell_row[:, h * LANES : (h + 1) * LANES]
            out[pl.ds(at + 49, 1), :] = live[:, h * LANES : (h + 1) * LANES]
            out[pl.ds(at + 50, 6), :] = jnp.zeros((6, LANES), F32)


def weight_map(cell_row, live):
    cell = cell_row.astype(jnp.int32)
    row, col = cell // NY, cell % NY
    nslot = cell.shape[1]
    on_col = (iota((NY, nslot), 0) == col).astype(jnp.bfloat16)
    on_row = iota((LV * RX, nslot), 0) == row
    total = jnp.zeros((LV * RX, NY), F32)
    rest = live
    for _ in range(3):
        part = rest.astype(jnp.bfloat16).astype(F32)
        rest = rest - part
        lhs = jnp.where(on_row, part, 0.0).astype(jnp.bfloat16)
        total += lax.dot_general(lhs, on_col, NT, preferred_element_type=F32)
    return total


def at(x, h, l):
    return pl.ds(pl.multiple_of(x * LINE + (h * LV + l) * NP, NP), NP)


def level_sum(c, l):
    if l == 0:
        return c[1]
    if l == LV - 1:
        return c[l - 1]
    return c[l - 1] + c[l + 1]


def slot_row(msg, r):
    return jnp.concatenate([msg[pl.ds(AUX + h * SIDE + r, 1), :] for h in range(2)], axis=1)


def tile_kernel(probes, wind, cells, weight, count, place, low, high, out, u, v, coef, wmap, ext):
    t, last = place[0, 0], place[0, 1] - 1
    lane = iota((NP, LANES), 1)
    first_lane, last_lane = lane == 0, lane == LANES - 1
    col = iota((ROWS, LANES), 1)
    for h in range(2):
        cols = pl.ds(h * LANES, LANES)
        for i in range(16):
            ext[i, pl.ds(HALO, RX), :] = wind[pl.ds(i * RX, RX), cols]
            ext[i, pl.ds(1, 3), :] = low[pl.ds(AUX + h * SIDE + 3 * i, 3), :]
            ext[i, pl.ds(HALO + RX, 3), :] = high[pl.ds(AUX + h * SIDE + 3 * i, 3), :]
        for k in range(2):
            for l in range(LV):
                a = 0.5 * ext[(k * 2 + 0) * LV + l]
                b = 0.5 * ext[(k * 2 + 1) * LV + l]
                plus, minus = 0.15 - b, 0.15 + b
                if h:
                    plus = jnp.where(col < LANES - 1, plus, 0.0)
                else:
                    minus = jnp.where(col > 0, minus, 0.0)
                for j, value in enumerate((0.15 - a, 0.15 + a, plus, minus)):
                    coef[(k * 4 + j) * LV + l, h] = value
    own = weight_map(cells[...].astype(F32), live_weights(weight, count))
    wlow = weight_map(slot_row(low, 48), slot_row(low, 49))
    whigh = weight_map(slot_row(high, 48), slot_row(high, 49))
    for h in range(2):
        cols = slice(h * LANES, (h + 1) * LANES)
        for l in range(LV):
            wmap[l, h, pl.ds(HALO, RX), :] = own[l * RX : (l + 1) * RX, cols]
            wmap[l, h, pl.ds(2, 2), :] = wlow[l * RX + RX - 2 : l * RX + RX, cols]
            wmap[l, h, pl.ds(HALO + RX, 2), :] = whigh[l * RX : l * RX + 2, cols]
    half = HALO * LINE
    u[pl.ds(0, half), :] = low[pl.ds(0, half), :]
    u[pl.ds(half + RX * LINE, half), :] = high[pl.ds(0, half), :]

    for x in range(RX):
        for h in range(2):
            for l in range(LV):
                u[at(x + HALO, h, l), :] = arrived(probes, x, h, l)

    def cf(k, j, l, h, x):
        return coef[(k * 4 + j) * LV + l, h, pl.ds(x, 1), :]

    def next_column(lo, hi, wrap):
        lo, hi = pltpu.roll(lo, LANES - 1, 1), pltpu.roll(hi, LANES - 1, 1)
        return jnp.where(last_lane, hi, lo), jnp.where(last_lane, lo, hi) if wrap else hi

    def previous_column(lo, hi, wrap):
        lo, hi = pltpu.roll(lo, 1, 1), pltpu.roll(hi, 1, 1)
        return jnp.where(first_lane, hi, lo) if wrap else lo, jnp.where(first_lane, lo, hi)

    def forward(src, k, x, put):
        c = [[src[at(x, h, l), :] for l in range(LV)] for h in range(2)]
        for l in range(LV):
            plus = next_column(c[0][l], c[1][l], False)
            minus = previous_column(c[0][l], c[1][l], False)
            for h in range(2):
                r = 0.2 * c[h][l] + 0.1 * level_sum(c[h], l)
                r += cf(k, 0, l, h, x) * src[at(x + 1, h, l), :]
                r += cf(k, 1, l, h, x) * src[at(x - 1, h, l), :]
                r += cf(k, 2, l, h, x) * plus[h]
                r += cf(k, 3, l, h, x) * minus[h]
                put(x, h, l, r)

    def adjoint(src, k, x, put):
        c = [[src[at(x, h, l), :] for l in range(LV)] for h in range(2)]
        for l in range(LV):
            plus = next_column(*(cf(k, 3, l, h, x) * c[h][l] for h in range(2)), True)
            minus = previous_column(*(cf(k, 2, l, h, x) * c[h][l] for h in range(2)), True)
            for h in range(2):
                r = 0.2 * c[h][l] + 0.1 * level_sum(c[h], l)
                r += cf(k, 1, l, h, x + 1) * src[at(x + 1, h, l), :]
                r += cf(k, 0, l, h, x - 1) * src[at(x - 1, h, l), :]
                put(x, h, l, r + plus[h] + minus[h])

    def sweep(lo, hi, op, src, k, put):
        def step(x, _):
            op(src, k, x, put)
            return 0

        lax.fori_loop(lo, hi, step, 0)

    def clear(dst, lo, hi):
        n = (hi - lo) * LINE
        dst[pl.ds(lo * LINE, n), :] = jnp.zeros((n, LANES), F32)

    def put_v(x, h, l, r):
        v[at(x, h, l), :] = r

    def put_weighted(x, h, l, r):
        u[at(x, h, l), :] = wmap[l, h, pl.ds(x, 1), :] * r

    def put_out(x, h, l, r):
        out[at(x - HALO, h, l), :] = r

    sweep(1, ROWS - 1, forward, u, 0, put_v)

    @pl.when(t == 0)
    def _():
        clear(v, 1, HALO)

    @pl.when(t == last)
    def _():
        clear(v, HALO + RX, ROWS - 1)

    sweep(2, ROWS - 2, forward, v, 1, put_weighted)
    sweep(3, ROWS - 3, adjoint, u, 1, put_v)

    @pl.when(t == 0)
    def _():
        clear(v, HALO - 1, HALO)

    @pl.when(t == last)
    def _():
        clear(v, HALO + RX, HALO + RX + 1)

    sweep(HALO, HALO + RX, adjoint, v, 0, put_out)


def all_blocks(t):
    return t + pltpu.roll(t, 32, 1) + pltpu.roll(t, 64, 1) + pltpu.roll(t, 96, 1)


def folded(prod):
    lane = iota((NP, 128), 1) // NP
    t = jnp.zeros((NP, 128), F32)
    for l in range(LV):
        t += jnp.where(lane == l, prod[l * NP : (l + 1) * NP], 0.0)
    return all_blocks(t)


def product(a, b, dims):
    return lax.dot_general(a, b, (dims, ((), ())), precision=HIGH, preferred_element_type=F32)


def gram_kernel(parts, probes, place, share, msg):
    o = place[0, 0]
    gram = jnp.zeros((BLK, BLK), F32)
    cross = jnp.zeros((BLK, BLK), F32)
    for h in range(2):
        s = parts[pl.ds(h * BLK, BLK), :]
        for g in range(1, 16):
            s = s + parts[pl.ds(g * LINE + h * BLK, BLK), :]
        share[pl.ds(h * BLK, BLK), :] = s
        omega = jnp.concatenate([arrived(probes, o, h, l) for l in range(LV)], axis=0)
        gram += product(s, s, ((1,), (1,)))
        cross += product(omega, s, ((1,), (1,)))
    gram, cross = folded(gram), folded(cross)
    shifted = pltpu.roll(cross, 16, 1)
    lane = iota((8, 128), 1)
    packed = jnp.zeros((8, 128), F32)
    for b in range(4):
        packed = jnp.where(lane // 32 == b, gram[8 * b : 8 * b + 8], packed)
    spare = (lane < 64) & (lane % 32 >= 16)
    for kind in range(4):
        rb, src = kind // 2, (cross if kind % 2 else shifted)
        piece = jnp.where(lane < 32, src[16 * rb : 16 * rb + 8], src[16 * rb + 8 : 16 * rb + 16])
        value = jnp.where(spare, piece, packed)
        for i in range(4):
            msg[pl.ds((4 * i + kind) * 8, 8), :] = value


def sum_kernel(parts, msg):
    n = parts.shape[0] // 8
    s = parts[pl.ds(0, 8), :]
    for g in range(1, n):
        s = s + parts[pl.ds(8 * g, 8), :]
    for d in range(msg.shape[0] // 8):
        msg[pl.ds(8 * d, 8), :] = s


def basis_kernel(parts, share, msg, *, scale):
    n = parts.shape[0] // 8
    s = parts[pl.ds(0, 8), :]
    for g in range(1, n):
        s = s + parts[pl.ds(8 * g, 8), :]
    lane8 = iota((8, 128), 1) // 32
    rows = [all_blocks(jnp.where(lane8 == b, s, 0.0)) for b in range(4)]
    gram = jnp.concatenate(rows, axis=0)
    square = jnp.concatenate([gram] * 4, axis=0)
    flipped = square.T[:NP]
    row, lane = iota((NP, 128), 0), iota((NP, 128), 1)
    a = jnp.where((row < 16) & (lane % 32 >= 16), flipped, gram)
    a = jnp.where(lane < NP, a, jnp.where(lane - NP == row, 1.0, 0.0))
    for j in range(NP - 1):
        pivot = a[j : j + 1, :]
        scaled = pivot / a[j : j + 1, j : j + 1]
        factor = jnp.where(row > j, a[:, j : j + 1], 0.0)
        a = a - factor * scaled
    diag = jnp.sum(jnp.where(lane == row, a, 0.0), axis=1, keepdims=True)
    inverse = jnp.where(lane // 32 == 1, a * (scale / jnp.sqrt(diag)), 0.0)
    inverse = all_blocks(inverse)
    r = iota((128, NP), 0)
    pick = (iota((128, NP), 1) == 2 * (r // 8) + r % 2).astype(F32)
    wide = product(pick, inverse, ((1,), (0,)))
    r = iota((128, 128), 0)
    wide = jnp.where(iota((128, 128), 1) // 32 == (r // 2) % 4, wide, 0.0)
    for h in range(2):
        rows = product(wide, share[pl.ds(h * BLK, BLK), :], ((1,), (0,)))
        for d in range(16):
            msg[pl.ds((3 * d + h) * 8, 8), :] = rows[8 * d : 8 * d + 8]
    for d in range(16):
        msg[pl.ds((3 * d + 2) * 8, 8), :] = s


def finish_kernel(got, basis, core, *, factor):
    for l in range(LV):
        for j in range(2):
            for h in range(2):
                basis[pl.ds((j * LV + l) * RX, RX), pl.ds(h * LANES, LANES)] = got[
                    pl.ds(h * 8 + 2 * l + j, RX, stride=24), :
                ]
    lane = iota((8, 128), 1)
    rows = []
    for rb in range(2):
        for half in range(2):
            first = 16 + 32 * half
            row = jnp.zeros((8, 128), F32)
            for cb in range(2):
                tile = got[pl.ds((3 * (2 * rb + cb) + 2) * 8, 8), :]
                moved = pltpu.roll(tile, (16 * cb - first) % 128, 1)
                row = jnp.where(lane // 16 == cb, moved, row)
            rows.append(row)
    core[...] = jnp.concatenate(rows, axis=0)[:, :NP] * factor


def shape(*dims):
    return jax.ShapeDtypeStruct(dims, F32)


def call(kernel, specs, outs, scratch=()):
    many = isinstance(outs, tuple)
    return pl.pallas_call(
        kernel,
        out_shape=outs,
        in_specs=specs,
        out_specs=(VM,) * len(outs) if many else VM,
        scratch_shapes=list(scratch),
    )


def on_device(probes, wind, station_cell, obs_count, obs_weight):
    tiles, groups = lax.axis_size("space"), lax.axis_size("obs")
    t, o = lax.axis_index("space"), lax.axis_index("obs")
    flat = probes.reshape(NP, LV, 2, 8, 2, LANES).transpose(0, 1, 2, 4, 3, 5).reshape(-1, LANES)
    winds = wind.reshape(16 * RX, NY)
    up, down = call(pack_kernel, [VM] * 4 + [SM], (shape(MSG, LANES), shape(MSG, LANES)))(
        flat, winds, station_cell, obs_weight, obs_count
    )
    low = lax.ppermute(up, "space", [(i, i + 1) for i in range(tiles - 1)])
    high = lax.ppermute(down, "space", [(i + 1, i) for i in range(tiles - 1)])
    place = jnp.stack([t, jnp.int32(tiles)]).reshape(1, 2).astype(jnp.int32)
    local = call(
        tile_kernel,
        [VM] * 4 + [SM, SM] + [VM] * 2,
        shape(RX * LINE, LANES),
        (
            pltpu.VMEM((ROWS * LINE, LANES), F32),
            pltpu.VMEM((ROWS * LINE, LANES), F32),
            pltpu.VMEM((32, 2, ROWS, LANES), F32),
            pltpu.VMEM((LV, 2, ROWS, LANES), F32),
            pltpu.VMEM((16, ROWS, LANES), F32),
        ),
    )(flat, winds, station_cell, obs_weight, obs_count, place, low, high)
    parts = lax.all_to_all(local.reshape(groups, LINE, LANES), "obs", 0, 0, tiled=True)
    share, msg = call(gram_kernel, [VM, VM, SM], (shape(LINE, LANES), shape(groups * 8, 128)))(
        parts.reshape(groups * LINE, LANES), flat, o.reshape(1, 1).astype(jnp.int32)
    )
    got = lax.all_to_all(msg.reshape(groups, 8, 128), "obs", 0, 0, tiled=True)
    msg = call(sum_kernel, [VM], shape(tiles * 8, 128))(got.reshape(groups * 8, 128))
    got = lax.all_to_all(msg.reshape(tiles, 8, 128), "space", 0, 0, tiled=True)
    scale = math.sqrt(LV * RX * tiles * NY)
    msg = call(
        lambda *refs: basis_kernel(*refs, scale=scale), [VM] * 2, shape(groups * 24, LANES)
    )(got.reshape(tiles * 8, 128), share)
    got = lax.all_to_all(msg.reshape(groups, 24, LANES), "obs", 0, 0, tiled=True)
    factor = 1.0 / (groups * tiles * station_cell.shape[1])
    basis, core = call(
        lambda *refs: finish_kernel(*refs, factor=factor),
        [VM],
        (shape(2 * LV * RX, NY), shape(NP, NP)),
    )(got.reshape(groups * 24, LANES))
    return basis.reshape(2, LV, RX, NY), core


def solution(mesh):
    in_specs = (
        P(None, None, "space", None),
        P("obs", None, None, None, "space", None),
        P("obs", "space"),
        P("obs", "space"),
        P("obs", "space"),
    )
    out_specs = (P("obs", None, "space", None), P())
    return jax.shard_map(
        on_device, mesh=mesh, in_specs=in_specs, out_specs=out_specs, check_vma=False
    )
```

```python
import math

import jax
import jax.numpy as jnp
from jax import lax
from jax.experimental import pallas as pl
from jax.experimental.pallas import tpu as pltpu
from jax.sharding import PartitionSpec as P

F32 = jnp.float32
HIGH = lax.Precision.HIGHEST
VM = pl.BlockSpec(memory_space=pltpu.VMEM)
SM = pl.BlockSpec(memory_space=pltpu.SMEM)
NT = (((1,), (1,)), ((), ()))

NP, LV, RX, NY = 32, 4, 16, 256
OWN = 16
WIN = 32
MARGIN = 8
HALO = 4
ROWS = RX + 2 * HALO
LANES = 128
PAD = 8
UNROLL = 4
KINDS = 5
SIDE = KINDS * LV * HALO
MSG = 2 * SIDE + NP * HALO


def iota(shape, dim):
    return lax.broadcasted_iota(jnp.int32, shape, dim)


def live_weights(weight_ref, count_ref):
    w = weight_ref[...]
    return jnp.where(iota(w.shape, 1) < count_ref[0, 0], w, 0.0)


def weight_map(cell_row, live):
    cell = cell_row.astype(jnp.int32)
    row, col = cell // NY, cell % NY
    nslot = cell.shape[1]
    on_col = (iota((NY, nslot), 0) == col).astype(jnp.bfloat16)
    on_row = iota((LV * RX, nslot), 0) == row
    total = jnp.zeros((LV * RX, NY), F32)
    rest = live
    for _ in range(3):
        part = rest.astype(jnp.bfloat16).astype(F32)
        rest = rest - part
        lhs = jnp.where(on_row, part, 0.0).astype(jnp.bfloat16)
        total += lax.dot_general(lhs, on_col, NT, preferred_element_type=F32)
    return total


def window(tiles, first):
    shape = tiles[0][0].shape
    lane = iota(shape, 1)
    col = first + lane % WIN
    halves = []
    for h in range(2):
        start = first - h * LANES
        if isinstance(first, int) and not (-WIN < start < LANES):
            halves.append(None)
            continue
        acc = jnp.zeros(shape, F32)
        for l in range(LV):
            shift = l * WIN - start
            shift = shift % LANES if isinstance(first, int) else (shift + 2 * LANES) % LANES
            acc = jnp.where(lane // WIN == l, pltpu.roll(tiles[l][h], shift, 1), acc)
        halves.append(acc)
    if halves[0] is None:
        value = halves[1]
    elif halves[1] is None:
        value = halves[0]
    else:
        value = jnp.where(col < LANES, halves[0], halves[1])
    return jnp.where((col >= 0) & (col < NY), value, 0.0)


def prepare_kernel(probes, wind, cells, weight, count, place, raw, patch, up, down):
    first = place[0, 2] * OWN - MARGIN
    for i in range(4 * LV):
        raw[pl.ds(i * RX, RX), :] = 0.5 * wind[pl.ds(i * RX, RX), :]
    raw[pl.ds(4 * LV * RX, LV * RX), :] = weight_map(
        cells[...].astype(F32), live_weights(weight, count)
    )

    def one(p, _):
        for xt in range(2):
            tiles = [
                [
                    probes[
                        pl.ds(pl.multiple_of((p * LV + l) * RX + 8 * xt, 8), 8),
                        pl.ds(h * LANES, LANES),
                    ]
                    for h in range(2)
                ]
                for l in range(LV)
            ]
            patch[pl.ds(pl.multiple_of(p * RX + 8 * xt, 8), 8), :] = window(tiles, first)
        return 0

    lax.fori_loop(0, NP, one, 0, unroll=2)
    for out, start in ((up, RX - HALO), (down, 0)):
        for h in range(2):
            for i in range(KINDS * LV):
                out[pl.ds(h * SIDE + i * HALO, HALO), :] = raw[
                    pl.ds(i * RX + start, HALO), pl.ds(h * LANES, LANES)
                ]
        for p in range(NP):
            out[pl.ds(2 * SIDE + p * HALO, HALO), :] = patch[pl.ds(p * RX + start, HALO), :]


def message_kernel(raw, low, high, msg, edge):
    for h in range(2):
        for i in range(KINDS * LV):
            src = pl.ds(h * SIDE + i * HALO, HALO)
            edge[i, h, pl.ds(0, HALO), :] = low[src, :]
            edge[i, h, pl.ds(HALO, HALO), :] = high[src, :]
    for kind in range(KINDS):
        for xt in range(3):
            tiles = [
                [
                    raw[
                        pl.ds((kind * LV + l) * RX + 8 * xt, 8), pl.ds(h * LANES, LANES)
                    ]
                    if xt < 2
                    else edge[kind * LV + l, h]
                    for h in range(2)
                ]
                for l in range(LV)
            ]
            for d in range(NY // OWN):
                value = window(tiles, d * OWN - MARGIN)
                base = (d * KINDS + kind) * ROWS
                if xt < 2:
                    msg[pl.ds(base + HALO + 8 * xt, 8), :] = value
                else:
                    msg[pl.ds(base, HALO), :] = value[:HALO]
                    msg[pl.ds(base + HALO + RX, HALO), :] = value[HALO:]


def all_blocks(t):
    return t + pltpu.roll(t, 32, 1) + pltpu.roll(t, 64, 1) + pltpu.roll(t, 96, 1)


def product(a, b, dims):
    return lax.dot_general(a, b, (dims, ((), ())), precision=HIGH, preferred_element_type=F32)


def aligned(row):
    return pl.multiple_of(row, 8)


def patch_kernel(
    got, patch, low, high, place, share, msg, u, au, dx, dy, cf, t1, t2, va, pa, qa, s
):
    t, tiles, o = place[0, 0], place[0, 1], place[0, 2]
    lane = iota((8, LANES), 1)
    plus_level = jnp.where(lane < LANES - WIN, 0.1, 0.0)
    minus_level = jnp.where(lane >= WIN, 0.1, 0.0)
    col = o * OWN - MARGIN + lane % WIN
    inside = []
    for i in range(3):
        row = t * RX - HALO + 8 * i + iota((8, LANES), 0)
        inside.append((row >= 0) & (row < tiles * RX) & (col >= 0) & (col < NY))

    def levels(c):
        return plus_level * pltpu.roll(c, LANES - WIN, 1) + minus_level * pltpu.roll(c, WIN, 1)

    def right(c):
        return pltpu.roll(c, LANES - 1, 1)

    def left(c):
        return pltpu.roll(c, 1, 1)

    edge = jnp.zeros((PAD, LANES), F32)
    for ref in (u, va, pa, qa):
        ref[pl.ds(0, PAD), :] = edge
        ref[pl.ds(PAD + NP * ROWS, PAD), :] = edge
    for j in range(4):
        cf[pl.ds(j * (ROWS + 2 * PAD), PAD), :] = edge
        cf[pl.ds(j * (ROWS + 2 * PAD) + PAD + ROWS, PAD), :] = edge
    for ref in (t1, t2):
        for j in range(UNROLL):
            ref[pl.ds(j * (ROWS + 2 * PAD), PAD), :] = edge
            ref[pl.ds(j * (ROWS + 2 * PAD) + PAD + ROWS, PAD), :] = edge
    for p in range(NP):
        base = PAD + p * ROWS
        u[pl.ds(base, HALO), :] = low[pl.ds(2 * SIDE + p * HALO, HALO), :]
        u[pl.ds(base + HALO, RX), :] = patch[pl.ds(p * RX, RX), :]
        u[pl.ds(base + HALO + RX, HALO), :] = high[pl.ds(2 * SIDE + p * HALO, HALO), :]

    def shared(p, _):
        for i in range(3):
            at = aligned(p * ROWS + 8 * i)
            c = u[pl.ds(at + PAD, 8), :]
            xp, xm = u[pl.ds(at + PAD + 1, 8), :], u[pl.ds(at + PAD - 1, 8), :]
            yp, ym = right(c), left(c)
            mean = 0.2 * c + 0.15 * ((xp + xm) + (yp + ym)) + levels(c)
            au[pl.ds(at, 8), :] = jnp.where(inside[i], mean, 0.0)
            dx[pl.ds(at, 8), :] = jnp.where(inside[i], xp - xm, 0.0)
            dy[pl.ds(at, 8), :] = jnp.where(inside[i], yp - ym, 0.0)
            for ref in (va, pa, qa):
                ref[pl.ds(at + PAD, 8), :] = edge
        return 0

    lax.fori_loop(0, NP, shared, 0, unroll=4)

    def coef(j, i, off=0):
        return cf[pl.ds(j * (ROWS + 2 * PAD) + PAD + 8 * i + off, 8), :]

    def one_window(g, _):
        base = g * (KINDS * ROWS)

        def of(kind, i):
            return got[pl.ds(aligned(base + kind * ROWS + 8 * i), 8), :]

        for i in range(3):
            a, b = of(2, i), of(3, i)
            for j, value in enumerate((0.15 - a, 0.15 + a, 0.15 - b, 0.15 + b)):
                cf[pl.ds(j * (ROWS + 2 * PAD) + PAD + 8 * i, 8), :] = value

        def some(step, _):
            slots = range(UNROLL)
            at = [[aligned((step * UNROLL + q) * ROWS + 8 * i) for i in range(3)] for q in slots]
            slot = [[q * (ROWS + 2 * PAD) + PAD + 8 * i for i in range(3)] for q in slots]
            for i in range(3):
                a, b = of(0, i), of(1, i)
                for q in slots:
                    here = pl.ds(at[q][i], 8)
                    t1[pl.ds(slot[q][i], 8), :] = au[here, :] - a * dx[here, :] - b * dy[here, :]
            for i in range(3):
                cxp, cxm, cyp, cym = (coef(j, i) for j in range(4))
                w = of(4, i)
                for q in slots:
                    c = t1[pl.ds(slot[q][i], 8), :]
                    r = 0.2 * c + levels(c)
                    r += cxp * t1[pl.ds(slot[q][i] + 1, 8), :]
                    r += cxm * t1[pl.ds(slot[q][i] - 1, 8), :]
                    r += cyp * right(c) + cym * left(c)
                    t2[pl.ds(slot[q][i], 8), :] = w * r
            for i in range(3):
                cxp, cxm, cyp, cym = coef(0, i, -1), coef(1, i, 1), coef(2, i), coef(3, i)
                a, b = of(0, i), of(1, i)
                for q in slots:
                    c = t2[pl.ds(slot[q][i], 8), :]
                    r = 0.2 * c + levels(c)
                    r += cxm * t2[pl.ds(slot[q][i] + 1, 8), :]
                    r += cxp * t2[pl.ds(slot[q][i] - 1, 8), :]
                    r += right(cym * c) + left(cyp * c)
                    here = pl.ds(at[q][i] + PAD, 8)
                    va[here, :] += r
                    pa[here, :] += a * r
                    qa[here, :] += b * r
            return 0

        lax.fori_loop(0, NP // UNROLL, some, 0)
        return 0

    lax.fori_loop(0, got.shape[0] // (KINDS * ROWS), one_window, 0)

    def mask(p, _):
        for i in range(3):
            at = pl.ds(aligned(PAD + p * ROWS + 8 * i), 8)
            for ref in (va, pa, qa):
                ref[at, :] = jnp.where(inside[i], ref[at, :], 0.0)
        return 0

    lax.fori_loop(0, NP, mask, 0, unroll=4)
    core_lane = (lane % WIN >= MARGIN) & (lane % WIN < MARGIN + OWN)

    def last(p, _):
        for i in range(2):
            at = aligned(PAD + p * ROWS + 8 * i) + HALO
            c, q = va[pl.ds(at, 8), :], qa[pl.ds(at, 8), :]
            r = 0.2 * c + levels(c)
            r += 0.15 * ((va[pl.ds(at + 1, 8), :] + va[pl.ds(at - 1, 8), :]) + (right(c) + left(c)))
            r += (pa[pl.ds(at + 1, 8), :] - pa[pl.ds(at - 1, 8), :]) + (right(q) - left(q))
            s[pl.ds(aligned(p * RX + 8 * i), 8), :] = jnp.where(core_lane, r, 0.0)
        return 0

    lax.fori_loop(0, NP, last, 0, unroll=4)

    gram = jnp.zeros((NP, LANES), F32)
    cross = jnp.zeros((NP, LANES), F32)
    for x in range(RX):
        sx = s[pl.ds(x, NP, stride=RX), :]
        share[pl.ds(x * NP, NP), :] = sx
        four = jnp.concatenate([sx] * 4, axis=0)
        gram += product(sx, four, ((1,), (1,)))
        cross += product(u[pl.ds(PAD + HALO + x, NP, stride=ROWS), :], four, ((1,), (1,)))
    shifted = pltpu.roll(cross, 16, 1)
    lane = iota((8, 128), 1)
    packed = jnp.zeros((8, 128), F32)
    for b in range(4):
        packed = jnp.where(lane // 32 == b, gram[8 * b : 8 * b + 8], packed)
    spare = (lane < 64) & (lane % 32 >= 16)
    for kind in range(4):
        rb, src = kind // 2, (cross if kind % 2 else shifted)
        piece = jnp.where(lane < 32, src[16 * rb : 16 * rb + 8], src[16 * rb + 8 : 16 * rb + 16])
        value = jnp.where(spare, piece, packed)
        for i in range(4):
            msg[pl.ds((4 * i + kind) * 8, 8), :] = value


def sum_kernel(parts, msg):
    n = parts.shape[0] // 8
    s = parts[pl.ds(0, 8), :]
    for g in range(1, n):
        s = s + parts[pl.ds(8 * g, 8), :]
    for d in range(msg.shape[0] // 8):
        msg[pl.ds(8 * d, 8), :] = s


def basis_kernel(parts, share, msg, *, scale):
    n = parts.shape[0] // 8
    s = parts[pl.ds(0, 8), :]
    for g in range(1, n):
        s = s + parts[pl.ds(8 * g, 8), :]
    lane8 = iota((8, 128), 1) // 32
    rows = [all_blocks(jnp.where(lane8 == b, s, 0.0)) for b in range(4)]
    gram = jnp.concatenate(rows, axis=0)
    square = jnp.concatenate([gram] * 4, axis=0)
    flipped = square.T[:NP]
    row, lane = iota((NP, 128), 0), iota((NP, 128), 1)
    a = jnp.where((row < 16) & (lane % 32 >= 16), flipped, gram)
    a = jnp.where(lane < NP, a, jnp.where(lane - NP == row, 1.0, 0.0))
    for j in range(NP - 1):
        pivot = a[j : j + 1, :]
        scaled = pivot / a[j : j + 1, j : j + 1]
        factor = jnp.where(row > j, a[:, j : j + 1], 0.0)
        a = a - factor * scaled
    diag = jnp.sum(jnp.where(lane == row, a, 0.0), axis=1, keepdims=True)
    inverse = jnp.where(lane // 32 == 1, a * (scale / jnp.sqrt(diag)), 0.0)
    inverse = all_blocks(inverse)
    r = iota((NP, NP), 0)
    pick = (iota((NP, NP), 1) == 2 * (r % 16) + r // 16).astype(F32)
    rows = product(pick, inverse, ((1,), (0,)))[:, :NP]
    mine = (lane[:16] % WIN >= MARGIN) & (lane[:16] % WIN < MARGIN + OWN)
    for x in range(RX):
        out = product(rows, share[pl.ds(x * NP, NP), :], ((1,), (0,)))
        both = jnp.where(mine, out[:16], pltpu.roll(out[16:], OWN, 1))
        msg[pl.ds(x, 16, stride=24), :] = both
    for d in range(16):
        msg[pl.ds(24 * d + 16, 8), :] = s


def finish_kernel(got, basis, core, *, factor):
    lane = iota((8, 128), 1)
    for xt in range(2):
        for h in range(2):
            sources = [got[pl.ds(24 * (8 * h + d) + 8 * xt, 8), :] for d in range(8)]
            for j in range(2):
                for l in range(LV):
                    acc = jnp.zeros((8, 128), F32)
                    for d in range(8):
                        shift = (OWN * d - WIN * l - MARGIN - OWN * j) % LANES
                        acc = jnp.where(lane // OWN == d, pltpu.roll(sources[d], shift, 1), acc)
                    basis[
                        pl.ds((j * LV + l) * RX + 8 * xt, 8), pl.ds(h * LANES, LANES)
                    ] = acc
    rows = []
    for rb in range(2):
        for half in range(2):
            first = 16 + 32 * half
            row = jnp.zeros((8, 128), F32)
            for cb in range(2):
                tile = got[pl.ds((3 * (2 * rb + cb) + 2) * 8, 8), :]
                moved = pltpu.roll(tile, (16 * cb - first) % 128, 1)
                row = jnp.where(lane // 16 == cb, moved, row)
            rows.append(row)
    core[...] = jnp.concatenate(rows, axis=0)[:, :NP] * factor


def shape(*dims):
    return jax.ShapeDtypeStruct(dims, F32)


def call(kernel, specs, outs, scratch=()):
    many = isinstance(outs, tuple)
    return pl.pallas_call(
        kernel,
        out_shape=outs,
        in_specs=specs,
        out_specs=(VM,) * len(outs) if many else VM,
        scratch_shapes=list(scratch),
    )


def on_device(probes, wind, station_cell, obs_count, obs_weight):
    tiles, groups = lax.axis_size("space"), lax.axis_size("obs")
    place = jnp.stack([lax.axis_index("space"), tiles, lax.axis_index("obs")])
    place = place.reshape(1, 3).astype(jnp.int32)
    raw, patch, up, down = call(
        prepare_kernel,
        [VM] * 4 + [SM] * 2,
        (
            shape(KINDS * LV * RX, NY),
            shape(NP * RX, LANES),
            shape(MSG, LANES),
            shape(MSG, LANES),
        ),
    )(
        probes.reshape(NP * LV * RX, NY),
        wind.reshape(4 * LV * RX, NY),
        station_cell,
        obs_weight,
        obs_count,
        place,
    )
    low = lax.ppermute(up, "space", [(i, i + 1) for i in range(tiles - 1)])
    high = lax.ppermute(down, "space", [(i + 1, i) for i in range(tiles - 1)])
    msg = call(
        message_kernel,
        [VM] * 3,
        shape(groups * KINDS * ROWS, LANES),
        (pltpu.VMEM((KINDS * LV, 2, 8, LANES), F32),),
    )(raw, low, high)
    got = lax.all_to_all(msg.reshape(groups, KINDS * ROWS, LANES), "obs", 0, 0, tiled=True)
    field = pltpu.VMEM((NP * ROWS, LANES), F32)
    padded = pltpu.VMEM((NP * ROWS + 2 * PAD, LANES), F32)
    share, msg = call(
        patch_kernel,
        [VM] * 4 + [SM],
        (shape(RX * NP, LANES), shape(groups * 8, 128)),
        (
            padded,
            field,
            field,
            field,
            pltpu.VMEM((4 * (ROWS + 2 * PAD), LANES), F32),
            pltpu.VMEM((UNROLL * (ROWS + 2 * PAD), LANES), F32),
            pltpu.VMEM((UNROLL * (ROWS + 2 * PAD), LANES), F32),
            padded,
            padded,
            padded,
            pltpu.VMEM((NP * RX, LANES), F32),
        ),
    )(got.reshape(groups * KINDS * ROWS, LANES), patch, low, high, place)
    got = lax.all_to_all(msg.reshape(groups, 8, 128), "obs", 0, 0, tiled=True)
    msg = call(sum_kernel, [VM], shape(tiles * 8, 128))(got.reshape(groups * 8, 128))
    got = lax.all_to_all(msg.reshape(tiles, 8, 128), "space", 0, 0, tiled=True)
    scale = math.sqrt(LV * RX * tiles * NY)
    msg = call(
        lambda *refs: basis_kernel(*refs, scale=scale), [VM] * 2, shape(groups * 24, LANES)
    )(got.reshape(tiles * 8, 128), share)
    got = lax.all_to_all(msg.reshape(groups, 24, LANES), "obs", 0, 0, tiled=True)
    factor = 1.0 / (groups * tiles * station_cell.shape[1])
    basis, core = call(
        lambda *refs: finish_kernel(*refs, factor=factor),
        [VM],
        (shape(2 * LV * RX, NY), shape(NP, NP)),
    )(got.reshape(groups * 24, LANES))
    return basis.reshape(2, LV, RX, NY), core


def solution(mesh):
    in_specs = (
        P(None, None, "space", None),
        P("obs", None, None, None, "space", None),
        P("obs", "space"),
        P("obs", "space"),
        P("obs", "space"),
    )
    out_specs = (P("obs", None, "space", None), P())
    return jax.shard_map(
        on_device, mesh=mesh, in_specs=in_specs, out_specs=out_specs, check_vma=False
    )
```

```python
import math

import jax
import jax.numpy as jnp
from jax import lax
from jax.experimental import pallas as pl
from jax.experimental.pallas import tpu as pltpu
from jax.sharding import PartitionSpec as P

F32 = jnp.float32
HIGH = lax.Precision.HIGHEST
VM = pl.BlockSpec(memory_space=pltpu.VMEM)
SM = pl.BlockSpec(memory_space=pltpu.SMEM)
NT = (((1,), (1,)), ((), ()))

NP, LV, RX, NY = 32, 4, 16, 256
OWN = 16
WIN = 32
MARGIN = 8
HALO = 4
ROWS = RX + 2 * HALO
LANES = 128
GROUP = LANES // WIN
PAD = 8
UNROLL = 4
SLOT = ROWS + 2 * PAD
KINDS = 5
SIDE = KINDS * LV * HALO
MSG = 2 * SIDE + NP * HALO


def iota(shape, dim):
    return lax.broadcasted_iota(jnp.int32, shape, dim)


def aligned(row):
    return pl.multiple_of(row, 8)


def live_weights(weight_ref, count_ref):
    w = weight_ref[...]
    return jnp.where(iota(w.shape, 1) < count_ref[0, 0], w, 0.0)


def weight_map(cell_row, live):
    cell = cell_row.astype(jnp.int32)
    row, col = cell // NY, cell % NY
    nslot = cell.shape[1]
    on_col = (iota((NY, nslot), 0) == col).astype(jnp.bfloat16)
    on_row = iota((LV * RX, nslot), 0) == row
    total = jnp.zeros((LV * RX, NY), F32)
    rest = live
    for _ in range(3):
        part = rest.astype(jnp.bfloat16).astype(F32)
        rest = rest - part
        lhs = jnp.where(on_row, part, 0.0).astype(jnp.bfloat16)
        total += lax.dot_general(lhs, on_col, NT, preferred_element_type=F32)
    return total


def window(tiles, first):
    shape = tiles[0][0].shape
    lane = iota(shape, 1)
    col = first + lane % WIN
    acc = None
    for k, (lo, hi) in enumerate(tiles):
        if isinstance(first, int) and first + WIN <= LANES:
            both = lo
        elif isinstance(first, int) and first >= LANES:
            both = hi
        else:
            both = jnp.where((lane >= first) & (lane < first + WIN), lo, hi)
        shift = k * WIN - first + 2 * LANES
        shift = shift % LANES if isinstance(first, int) else lax.rem(shift, LANES)
        both = pltpu.roll(both, shift, 1)
        acc = both if acc is None else jnp.where(lane // WIN == k, both, acc)
    return jnp.where((col >= 0) & (col < NY), acc, 0.0)


def prepare_kernel(probes, wind, cells, weight, count, place, raw, patch, up, down):
    first = place[0, 2] * OWN - MARGIN
    for i in range(4 * LV):
        raw[pl.ds(i * RX, RX), :] = 0.5 * wind[pl.ds(i * RX, RX), :]
    raw[pl.ds(4 * LV * RX, LV * RX), :] = weight_map(
        cells[...].astype(F32), live_weights(weight, count)
    )

    def one(p, _):
        for l in range(LV):
            for xt in range(2):
                tiles = [
                    [
                        probes[
                            pl.ds(aligned(((p * GROUP + k) * LV + l) * RX + 8 * xt), 8),
                            pl.ds(h * LANES, LANES),
                        ]
                        for h in range(2)
                    ]
                    for k in range(GROUP)
                ]
                patch[pl.ds(aligned((p * LV + l) * RX + 8 * xt), 8), :] = window(tiles, first)
        return 0

    lax.fori_loop(0, NP // GROUP, one, 0)
    for out, start in ((up, RX - HALO), (down, 0)):
        for h in range(2):
            for i in range(KINDS * LV):
                out[pl.ds(h * SIDE + i * HALO, HALO), :] = raw[
                    pl.ds(i * RX + start, HALO), pl.ds(h * LANES, LANES)
                ]
        for p in range(NP):
            out[pl.ds(2 * SIDE + p * HALO, HALO), :] = patch[pl.ds(p * RX + start, HALO), :]


def message_kernel(raw, low, high, msg, edge):
    for h in range(2):
        for i in range(KINDS * LV):
            src = pl.ds(h * SIDE + i * HALO, HALO)
            edge[i, h, pl.ds(0, HALO), :] = low[src, :]
            edge[i, h, pl.ds(HALO, HALO), :] = high[src, :]
    for kind in range(KINDS):
        for xt in range(3):
            tiles = [
                [
                    raw[
                        pl.ds((kind * LV + l) * RX + 8 * xt, 8), pl.ds(h * LANES, LANES)
                    ]
                    if xt < 2
                    else edge[kind * LV + l, h]
                    for h in range(2)
                ]
                for l in range(LV)
            ]
            for d in range(NY // OWN):
                value = window(tiles, d * OWN - MARGIN)
                base = (d * KINDS + kind) * ROWS
                if xt < 2:
                    msg[pl.ds(base + HALO + 8 * xt, 8), :] = value
                else:
                    msg[pl.ds(base, HALO), :] = value[:HALO]
                    msg[pl.ds(base + HALO + RX, HALO), :] = value[HALO:]


def all_blocks(t):
    return t + pltpu.roll(t, 32, 1) + pltpu.roll(t, 64, 1) + pltpu.roll(t, 96, 1)


def product(a, b, dims):
    return lax.dot_general(a, b, (dims, ((), ())), precision=HIGH, preferred_element_type=F32)


def level_sum(c, l):
    if l == 0:
        return c[1]
    if l == LV - 1:
        return c[l - 1]
    return c[l - 1] + c[l + 1]


def swap_groups(v):
    lane = iota(v[0].shape, 1)
    low, even = lane < 64, lane // 32 % 2 == 0

    def half(w):
        return pltpu.roll(w, 64, 1)

    x = [
        jnp.where(low, v[0], half(v[2])),
        jnp.where(low, v[1], half(v[3])),
        jnp.where(low, half(v[0]), v[2]),
        jnp.where(low, half(v[1]), v[3]),
    ]
    out = []
    for a in (0, 2):
        out.append(jnp.where(even, x[a], pltpu.roll(x[a + 1], 32, 1)))
        out.append(jnp.where(even, pltpu.roll(x[a], 96, 1), x[a + 1]))
    return out


def patch_kernel(
    got, patch, low, high, place, share, msg, u, au, dx, dy, cf, t1, t2, va, pa, qa, s, om
):
    t, tiles, o = place[0, 0], place[0, 1], place[0, 2]
    lane = iota((8, LANES), 1)
    col = o * OWN - MARGIN + lane % WIN
    inside = []
    for i in range(3):
        row = t * RX - HALO + 8 * i + iota((8, LANES), 0)
        inside.append((row >= 0) & (row < tiles * RX) & (col >= 0) & (col < NY))

    def right(c):
        return pltpu.roll(c, LANES - 1, 1)

    def left(c):
        return pltpu.roll(c, 1, 1)

    def levels(c, l):
        return 0.2 * c[l] + 0.1 * level_sum(c, l)

    edge = jnp.zeros((PAD, LANES), F32)
    for ref in (u, va, pa, qa):
        ref[pl.ds(0, PAD), :] = edge
        ref[pl.ds(PAD + NP * ROWS, PAD), :] = edge
    for ref, n in ((cf, 2 * LV), (t1, UNROLL * LV), (t2, UNROLL * LV)):
        for j in range(n):
            ref[pl.ds(j * SLOT, PAD), :] = edge
            ref[pl.ds(j * SLOT + PAD + ROWS, PAD), :] = edge
    for f in range(NP):
        base = PAD + f * ROWS
        u[pl.ds(base, HALO), :] = low[pl.ds(2 * SIDE + f * HALO, HALO), :]
        u[pl.ds(base + HALO, RX), :] = patch[pl.ds(f * RX, RX), :]
        u[pl.ds(base + HALO + RX, HALO), :] = high[pl.ds(2 * SIDE + f * HALO, HALO), :]

    def shared(p, _):
        for i in range(3):
            at = [aligned((p * LV + l) * ROWS + 8 * i) for l in range(LV)]
            c = [u[pl.ds(at[l] + PAD, 8), :] for l in range(LV)]
            for l in range(LV):
                xp, xm = u[pl.ds(at[l] + PAD + 1, 8), :], u[pl.ds(at[l] + PAD - 1, 8), :]
                yp, ym = right(c[l]), left(c[l])
                mean = levels(c, l) + 0.15 * ((xp + xm) + (yp + ym))
                here = pl.ds(at[l], 8)
                au[here, :] = jnp.where(inside[i], mean, 0.0)
                dx[here, :] = jnp.where(inside[i], xp - xm, 0.0)
                dy[here, :] = jnp.where(inside[i], yp - ym, 0.0)
                for ref in (va, pa, qa):
                    ref[pl.ds(at[l] + PAD, 8), :] = edge
        return 0

    lax.fori_loop(0, NP // GROUP, shared, 0)

    def coef(j, l, i, off=0):
        return cf[pl.ds((j * LV + l) * SLOT + PAD + 8 * i + off, 8), :]

    def one_window(g, _):
        base = g * (KINDS * ROWS)
        for i in range(3):
            for kind in range(KINDS):
                tile = got[pl.ds(aligned(base + kind * ROWS + 8 * i), 8), :]
                for l in range(LV):
                    m = jnp.take_along_axis(tile, l * WIN + lane % WIN, axis=1)
                    if kind in (2, 3):
                        pair = ((2 * kind - 4, 0.15 - m), (2 * kind - 3, 0.15 + m))
                    else:
                        pair = (({0: 4, 1: 5, 4: 6}[kind], m),)
                    for j, value in pair:
                        cf[pl.ds((j * LV + l) * SLOT + PAD + 8 * i, 8), :] = value

        def some(step, _):
            slots = range(UNROLL)

            def at(q, l, i):
                return aligned(((step * UNROLL + q) * LV + l) * ROWS + 8 * i)

            def slot(q, l, i, off=0):
                return pl.ds((q * LV + l) * SLOT + PAD + 8 * i + off, 8)

            for i in range(3):
                for l in range(LV):
                    a, b = coef(4, l, i), coef(5, l, i)
                    for q in slots:
                        here = pl.ds(at(q, l, i), 8)
                        t1[slot(q, l, i), :] = au[here, :] - a * dx[here, :] - b * dy[here, :]
            for i in range(3):
                c = [[t1[slot(q, l, i), :] for l in range(LV)] for q in slots]
                for l in range(LV):
                    cxp, cxm, cyp, cym = (coef(j, l, i) for j in range(4))
                    w = coef(6, l, i)
                    for q in slots:
                        r = levels(c[q], l)
                        r += cxp * t1[slot(q, l, i, 1), :] + cxm * t1[slot(q, l, i, -1), :]
                        r += cyp * right(c[q][l]) + cym * left(c[q][l])
                        t2[slot(q, l, i), :] = w * r
            for i in range(3):
                c = [[t2[slot(q, l, i), :] for l in range(LV)] for q in slots]
                for l in range(LV):
                    cxp, cxm = coef(0, l, i, -1), coef(1, l, i, 1)
                    cyp, cym = coef(2, l, i), coef(3, l, i)
                    a, b = coef(4, l, i), coef(5, l, i)
                    for q in slots:
                        r = levels(c[q], l)
                        r += cxm * t2[slot(q, l, i, 1), :] + cxp * t2[slot(q, l, i, -1), :]
                        r += right(cym * c[q][l]) + left(cyp * c[q][l])
                        here = pl.ds(at(q, l, i) + PAD, 8)
                        va[here, :] += r
                        pa[here, :] += a * r
                        qa[here, :] += b * r
            return 0

        lax.fori_loop(0, NP // GROUP // UNROLL, some, 0)
        return 0

    lax.fori_loop(0, got.shape[0] // (KINDS * ROWS), one_window, 0)

    def mask(f, _):
        for i in range(3):
            at = pl.ds(aligned(PAD + f * ROWS + 8 * i), 8)
            for ref in (va, pa, qa):
                ref[at, :] = jnp.where(inside[i], ref[at, :], 0.0)
        return 0

    lax.fori_loop(0, NP, mask, 0, unroll=4)
    core_lane = (lane % WIN >= MARGIN) & (lane % WIN < MARGIN + OWN)

    def last(p, _):
        for i in range(2):
            at = [aligned(PAD + (p * LV + l) * ROWS + 8 * i) + HALO for l in range(LV)]
            c = [va[pl.ds(at[l], 8), :] for l in range(LV)]
            done = []
            for l in range(LV):
                q = qa[pl.ds(at[l], 8), :]
                r = levels(c, l)
                xs = va[pl.ds(at[l] + 1, 8), :] + va[pl.ds(at[l] - 1, 8), :]
                r += 0.15 * (xs + (right(c[l]) + left(c[l])))
                r += (pa[pl.ds(at[l] + 1, 8), :] - pa[pl.ds(at[l] - 1, 8), :]) + (
                    right(q) - left(q)
                )
                done.append(jnp.where(core_lane, r, 0.0))
            for ref, values in (
                (s, swap_groups(done)),
                (om, swap_groups([u[pl.ds(at[l], 8), :] for l in range(LV)])),
            ):
                for k in range(GROUP):
                    ref[pl.ds(aligned((p * GROUP + k) * RX + 8 * i), 8), :] = values[k]
        return 0

    lax.fori_loop(0, NP // GROUP, last, 0)

    both = jnp.zeros((2 * NP, NP), F32)
    for x in range(RX):
        sx = s[pl.ds(x, NP, stride=RX), :]
        share[pl.ds(x * NP, NP), :] = sx
        rows = jnp.concatenate([sx, om[pl.ds(x, NP, stride=RX), :]], axis=0)
        both += product(rows, sx, ((1,), (1,)))
    spread = (iota((NP, LANES), 1) % NP == iota((NP, LANES), 0)).astype(F32)
    both = product(both, spread, ((1,), (0,)))
    gram, cross = both[:NP], both[NP:]
    shifted = pltpu.roll(cross, 16, 1)
    lane = iota((8, 128), 1)
    packed = jnp.zeros((8, 128), F32)
    for b in range(4):
        packed = jnp.where(lane // 32 == b, gram[8 * b : 8 * b + 8], packed)
    spare = (lane < 64) & (lane % 32 >= 16)
    for kind in range(4):
        rb, src = kind // 2, (cross if kind % 2 else shifted)
        piece = jnp.where(lane < 32, src[16 * rb : 16 * rb + 8], src[16 * rb + 8 : 16 * rb + 16])
        value = jnp.where(spare, piece, packed)
        for i in range(4):
            msg[pl.ds((4 * i + kind) * 8, 8), :] = value


def sum_kernel(parts, msg):
    n = parts.shape[0] // 8
    s = parts[pl.ds(0, 8), :]
    for g in range(1, n):
        s = s + parts[pl.ds(8 * g, 8), :]
    for d in range(msg.shape[0] // 8):
        msg[pl.ds(8 * d, 8), :] = s


def basis_kernel(parts, share, msg, *, scale):
    n = parts.shape[0] // 8
    s = parts[pl.ds(0, 8), :]
    for g in range(1, n):
        s = s + parts[pl.ds(8 * g, 8), :]
    lane8 = iota((8, 128), 1) // 32
    rows = [all_blocks(jnp.where(lane8 == b, s, 0.0)) for b in range(4)]
    gram = jnp.concatenate(rows, axis=0)
    square = jnp.concatenate([gram] * 4, axis=0)
    flipped = square.T[:NP]
    row, lane = iota((NP, 128), 0), iota((NP, 128), 1)
    a = jnp.where((row < 16) & (lane % 32 >= 16), flipped, gram)
    a = jnp.where(lane < NP, a, jnp.where(lane - NP == row, 1.0, 0.0))
    for j in range(NP - 1):
        pivot = a[j : j + 1, :]
        scaled = pivot / a[j : j + 1, j : j + 1]
        factor = jnp.where(row > j, a[:, j : j + 1], 0.0)
        a = a - factor * scaled
    diag = jnp.sum(jnp.where(lane == row, a, 0.0), axis=1, keepdims=True)
    inverse = jnp.where(lane // 32 == 1, a * (scale / jnp.sqrt(diag)), 0.0)
    inverse = all_blocks(inverse)
    r = iota((NP, NP), 0)
    pick = (iota((NP, NP), 1) == 2 * (r % 16) + r // 16).astype(F32)
    rows = product(pick, inverse, ((1,), (0,)))[:, :NP]
    mine = (lane[:16] % WIN >= MARGIN) & (lane[:16] % WIN < MARGIN + OWN)
    for x in range(RX):
        out = product(rows, share[pl.ds(x * NP, NP), :], ((1,), (0,)))
        both = jnp.where(mine, out[:16], pltpu.roll(out[16:], OWN, 1))
        msg[pl.ds(x, 16, stride=24), :] = both
    for d in range(16):
        msg[pl.ds(24 * d + 16, 8), :] = s


def finish_kernel(got, basis, core, *, factor):
    lane = iota((8, 128), 1)
    for xt in range(2):
        for h in range(2):
            sources = [got[pl.ds(24 * (8 * h + d) + 8 * xt, 8), :] for d in range(8)]
            for j in range(2):
                for l in range(LV):
                    acc = jnp.zeros((8, 128), F32)
                    for d in range(8):
                        shift = (OWN * d - WIN * l - MARGIN - OWN * j) % LANES
                        acc = jnp.where(lane // OWN == d, pltpu.roll(sources[d], shift, 1), acc)
                    basis[
                        pl.ds((j * LV + l) * RX + 8 * xt, 8), pl.ds(h * LANES, LANES)
                    ] = acc
    rows = []
    for rb in range(2):
        for half in range(2):
            first = 16 + 32 * half
            row = jnp.zeros((8, 128), F32)
            for cb in range(2):
                tile = got[pl.ds((3 * (2 * rb + cb) + 2) * 8, 8), :]
                moved = pltpu.roll(tile, (16 * cb - first) % 128, 1)
                row = jnp.where(lane // 16 == cb, moved, row)
            rows.append(row)
    core[...] = jnp.concatenate(rows, axis=0)[:, :NP] * factor


def shape(*dims):
    return jax.ShapeDtypeStruct(dims, F32)


def call(kernel, specs, outs, scratch=()):
    many = isinstance(outs, tuple)
    return pl.pallas_call(
        kernel,
        out_shape=outs,
        in_specs=specs,
        out_specs=(VM,) * len(outs) if many else VM,
        scratch_shapes=list(scratch),
    )


def on_device(probes, wind, station_cell, obs_count, obs_weight):
    tiles, groups = lax.axis_size("space"), lax.axis_size("obs")
    place = jnp.stack([lax.axis_index("space"), tiles, lax.axis_index("obs")])
    place = place.reshape(1, 3).astype(jnp.int32)
    raw, patch, up, down = call(
        prepare_kernel,
        [VM] * 4 + [SM] * 2,
        (
            shape(KINDS * LV * RX, NY),
            shape(NP * RX, LANES),
            shape(MSG, LANES),
            shape(MSG, LANES),
        ),
    )(
        probes.reshape(NP * LV * RX, NY),
        wind.reshape(4 * LV * RX, NY),
        station_cell,
        obs_weight,
        obs_count,
        place,
    )
    low = lax.ppermute(up, "space", [(i, i + 1) for i in range(tiles - 1)])
    high = lax.ppermute(down, "space", [(i + 1, i) for i in range(tiles - 1)])
    msg = call(
        message_kernel,
        [VM] * 3,
        shape(groups * KINDS * ROWS, LANES),
        (pltpu.VMEM((KINDS * LV, 2, 8, LANES), F32),),
    )(raw, low, high)
    got = lax.all_to_all(msg.reshape(groups, KINDS * ROWS, LANES), "obs", 0, 0, tiled=True)
    field = pltpu.VMEM((NP * ROWS, LANES), F32)
    padded = pltpu.VMEM((NP * ROWS + 2 * PAD, LANES), F32)
    share, msg = call(
        patch_kernel,
        [VM] * 4 + [SM],
        (shape(RX * NP, LANES), shape(groups * 8, 128)),
        (
            padded,
            field,
            field,
            field,
            pltpu.VMEM((7 * LV * SLOT, LANES), F32),
            pltpu.VMEM((UNROLL * LV * SLOT, LANES), F32),
            pltpu.VMEM((UNROLL * LV * SLOT, LANES), F32),
            padded,
            padded,
            padded,
            pltpu.VMEM((NP * RX, LANES), F32),
            pltpu.VMEM((NP * RX, LANES), F32),
        ),
    )(got.reshape(groups * KINDS * ROWS, LANES), patch, low, high, place)
    got = lax.all_to_all(msg.reshape(groups, 8, 128), "obs", 0, 0, tiled=True)
    msg = call(sum_kernel, [VM], shape(tiles * 8, 128))(got.reshape(groups * 8, 128))
    got = lax.all_to_all(msg.reshape(tiles, 8, 128), "space", 0, 0, tiled=True)
    scale = math.sqrt(LV * RX * tiles * NY)
    msg = call(
        lambda *refs: basis_kernel(*refs, scale=scale), [VM] * 2, shape(groups * 24, LANES)
    )(got.reshape(tiles * 8, 128), share)
    got = lax.all_to_all(msg.reshape(groups, 24, LANES), "obs", 0, 0, tiled=True)
    factor = 1.0 / (groups * tiles * station_cell.shape[1])
    basis, core = call(
        lambda *refs: finish_kernel(*refs, factor=factor),
        [VM],
        (shape(2 * LV * RX, NY), shape(NP, NP)),
    )(got.reshape(groups * 24, LANES))
    return basis.reshape(2, LV, RX, NY), core


def solution(mesh):
    in_specs = (
        P(None, None, "space", None),
        P("obs", None, None, None, "space", None),
        P("obs", "space"),
        P("obs", "space"),
        P("obs", "space"),
    )
    out_specs = (P("obs", None, "space", None), P())
    return jax.shard_map(
        on_device, mesh=mesh, in_specs=in_specs, out_specs=out_specs, check_vma=False
    )
```

```python
import math

import jax
import jax.numpy as jnp
from jax import lax
from jax.experimental import pallas as pl
from jax.experimental.pallas import tpu as pltpu
from jax.sharding import PartitionSpec as P

F32 = jnp.float32
HIGH = lax.Precision.HIGHEST
VM = pl.BlockSpec(memory_space=pltpu.VMEM)
SM = pl.BlockSpec(memory_space=pltpu.SMEM)
NT = (((1,), (1,)), ((), ()))

NP, LV, RX, NY = 32, 4, 16, 256
OWN = 16
WIN = 32
MARGIN = 8
HALO = 4
ROWS = RX + 2 * HALO
LANES = 128
GROUP = LANES // WIN
PAD = 8
UNROLL = 4
SLOT = ROWS + 2 * PAD
KINDS = 5
SIDE = KINDS * LV * HALO
MSG = 2 * SIDE + NP * HALO


def iota(shape, dim):
    return lax.broadcasted_iota(jnp.int32, shape, dim)


def aligned(row):
    return pl.multiple_of(row, 8)


def live_weights(weight_ref, count_ref):
    w = weight_ref[...]
    return jnp.where(iota(w.shape, 1) < count_ref[0, 0], w, 0.0)


def weight_map(cell_row, live):
    cell = cell_row.astype(jnp.int32)
    row, col = cell // NY, cell % NY
    nslot = cell.shape[1]
    on_col = (iota((NY, nslot), 0) == col).astype(jnp.bfloat16)
    on_row = iota((LV * RX, nslot), 0) == row
    total = jnp.zeros((LV * RX, NY), F32)
    rest = live
    for _ in range(3):
        part = rest.astype(jnp.bfloat16).astype(F32)
        rest = rest - part
        lhs = jnp.where(on_row, part, 0.0).astype(jnp.bfloat16)
        total += lax.dot_general(lhs, on_col, NT, preferred_element_type=F32)
    return total


def window(tiles, first):
    shape = tiles[0][0].shape
    lane = iota(shape, 1)
    col = first + lane % WIN
    acc = None
    for k, (lo, hi) in enumerate(tiles):
        if isinstance(first, int) and first + WIN <= LANES:
            both = lo
        elif isinstance(first, int) and first >= LANES:
            both = hi
        else:
            both = jnp.where((lane >= first) & (lane < first + WIN), lo, hi)
        shift = k * WIN - first + 2 * LANES
        shift = shift % LANES if isinstance(first, int) else lax.rem(shift, LANES)
        both = pltpu.roll(both, shift, 1)
        acc = both if acc is None else jnp.where(lane // WIN == k, both, acc)
    return jnp.where((col >= 0) & (col < NY), acc, 0.0)


def prepare_kernel(probes, wind, cells, weight, count, raw, patch, up, down):
    first = lax.axis_index("obs") * OWN - MARGIN
    for i in range(4 * LV):
        raw[pl.ds(i * RX, RX), :] = 0.5 * wind[pl.ds(i * RX, RX), :]
    raw[pl.ds(4 * LV * RX, LV * RX), :] = weight_map(
        cells[...].astype(F32), live_weights(weight, count)
    )

    def one(p, _):
        for l in range(LV):
            for xt in range(2):
                tiles = [
                    [
                        probes[
                            pl.ds(aligned(((p * GROUP + k) * LV + l) * RX + 8 * xt), 8),
                            pl.ds(h * LANES, LANES),
                        ]
                        for h in range(2)
                    ]
                    for k in range(GROUP)
                ]
                patch[pl.ds(aligned((p * LV + l) * RX + 8 * xt), 8), :] = window(tiles, first)
        return 0

    lax.fori_loop(0, NP // GROUP, one, 0)
    for out, start in ((up, RX - HALO), (down, 0)):
        for h in range(2):
            for i in range(KINDS * LV):
                out[pl.ds(h * SIDE + i * HALO, HALO), :] = raw[
                    pl.ds(i * RX + start, HALO), pl.ds(h * LANES, LANES)
                ]
        for p in range(NP):
            out[pl.ds(2 * SIDE + p * HALO, HALO), :] = patch[pl.ds(p * RX + start, HALO), :]


def own_kernel(raw, own):
    for kind in range(KINDS):
        for xt in range(2):
            tiles = [
                [
                    raw[pl.ds((kind * LV + l) * RX + 8 * xt, 8), pl.ds(h * LANES, LANES)]
                    for h in range(2)
                ]
                for l in range(LV)
            ]
            for d in range(NY // OWN):
                own[pl.ds((d * KINDS + kind) * RX + 8 * xt, 8), :] = window(
                    tiles, d * OWN - MARGIN
                )


def message_kernel(own, low, high, msg, edge):
    for h in range(2):
        for i in range(KINDS * LV):
            src = pl.ds(h * SIDE + i * HALO, HALO)
            edge[i, h, pl.ds(0, HALO), :] = low[src, :]
            edge[i, h, pl.ds(HALO, HALO), :] = high[src, :]
    for kind in range(KINDS):
        tiles = [[edge[kind * LV + l, h] for h in range(2)] for l in range(LV)]
        for d in range(NY // OWN):
            value = window(tiles, d * OWN - MARGIN)
            base = (d * KINDS + kind) * ROWS
            msg[pl.ds(base, HALO), :] = value[:HALO]
            msg[pl.ds(base + HALO, RX), :] = own[pl.ds((d * KINDS + kind) * RX, RX), :]
            msg[pl.ds(base + HALO + RX, HALO), :] = value[HALO:]


def all_blocks(t):
    return t + pltpu.roll(t, 32, 1) + pltpu.roll(t, 64, 1) + pltpu.roll(t, 96, 1)


def product(a, b, dims):
    return lax.dot_general(a, b, (dims, ((), ())), precision=HIGH, preferred_element_type=F32)


def level_sum(c, l):
    if l == 0:
        return c[1]
    if l == LV - 1:
        return c[l - 1]
    return c[l - 1] + c[l + 1]


def swap_groups(v):
    lane = iota(v[0].shape, 1)
    low, even = lane < 64, lane // 32 % 2 == 0

    def half(w):
        return pltpu.roll(w, 64, 1)

    x = [
        jnp.where(low, v[0], half(v[2])),
        jnp.where(low, v[1], half(v[3])),
        jnp.where(low, half(v[0]), v[2]),
        jnp.where(low, half(v[1]), v[3]),
    ]
    out = []
    for a in (0, 2):
        out.append(jnp.where(even, x[a], pltpu.roll(x[a + 1], 32, 1)))
        out.append(jnp.where(even, pltpu.roll(x[a], 96, 1), x[a + 1]))
    return out


def patch_kernel(
    got, patch, low, high, share, msg, u, au, dx, dy, cf, t1, t2, va, pa, qa, s, om
):
    t, o = lax.axis_index("space"), lax.axis_index("obs")
    tiles = lax.axis_size("space")
    lane = iota((8, LANES), 1)
    col = o * OWN - MARGIN + lane % WIN
    inside = []
    for i in range(3):
        row = t * RX - HALO + 8 * i + iota((8, LANES), 0)
        inside.append((row >= 0) & (row < tiles * RX) & (col >= 0) & (col < NY))

    def right(c):
        return pltpu.roll(c, LANES - 1, 1)

    def left(c):
        return pltpu.roll(c, 1, 1)

    def levels(c, l):
        return 0.2 * c[l] + 0.1 * level_sum(c, l)

    def tenfold(c, l):
        return (c[l] + c[l]) + level_sum(c, l)

    edge = jnp.zeros((PAD, LANES), F32)
    for ref in (u, va, pa, qa):
        ref[pl.ds(0, PAD), :] = edge
        ref[pl.ds(PAD + NP * ROWS, PAD), :] = edge
    for ref, n in ((cf, 2 * LV), (t1, UNROLL * LV), (t2, UNROLL * LV)):
        for j in range(n):
            ref[pl.ds(j * SLOT, PAD), :] = edge
            ref[pl.ds(j * SLOT + PAD + ROWS, PAD), :] = edge
    for f in range(NP):
        base = PAD + f * ROWS
        u[pl.ds(base, HALO), :] = low[pl.ds(2 * SIDE + f * HALO, HALO), :]
        u[pl.ds(base + HALO, RX), :] = patch[pl.ds(f * RX, RX), :]
        u[pl.ds(base + HALO + RX, HALO), :] = high[pl.ds(2 * SIDE + f * HALO, HALO), :]

    def shared(p, _):
        for i in range(3):
            at = [aligned((p * LV + l) * ROWS + 8 * i) for l in range(LV)]
            c = [u[pl.ds(at[l] + PAD, 8), :] for l in range(LV)]
            for l in range(LV):
                xp, xm = u[pl.ds(at[l] + PAD + 1, 8), :], u[pl.ds(at[l] + PAD - 1, 8), :]
                yp, ym = right(c[l]), left(c[l])
                mean = 0.01 * tenfold(c, l) + 0.015 * ((xp + xm) + (yp + ym))
                here = pl.ds(at[l], 8)
                au[here, :] = jnp.where(inside[i], mean, 0.0)
                dx[here, :] = jnp.where(inside[i], 0.1 * (xp - xm), 0.0)
                dy[here, :] = jnp.where(inside[i], 0.1 * (yp - ym), 0.0)
                for ref in (va, pa, qa):
                    ref[pl.ds(at[l] + PAD, 8), :] = edge
        return 0

    lax.fori_loop(0, NP // GROUP, shared, 0)

    def coef(j, l, i, off=0):
        return cf[pl.ds((j * LV + l) * SLOT + PAD + 8 * i + off, 8), :]

    def one_window(g, _):
        base = g * (KINDS * ROWS)
        for i in range(3):
            for kind in range(KINDS):
                tile = got[pl.ds(aligned(base + kind * ROWS + 8 * i), 8), :]
                for l in range(LV):
                    m = jnp.take_along_axis(tile, l * WIN + lane % WIN, axis=1)
                    if kind in (2, 3):
                        m = 10.0 * m
                        pair = ((2 * kind - 4, 1.5 - m), (2 * kind - 3, 1.5 + m))
                    else:
                        pair = (({0: 4, 1: 5, 4: 6}[kind], 0.1 * m if kind == 4 else m),)
                    for j, value in pair:
                        cf[pl.ds((j * LV + l) * SLOT + PAD + 8 * i, 8), :] = value

        def some(step, _):
            slots = range(UNROLL)

            def at(q, l, i):
                return aligned(((step * UNROLL + q) * LV + l) * ROWS + 8 * i)

            def slot(q, l, i, off=0):
                return pl.ds((q * LV + l) * SLOT + PAD + 8 * i + off, 8)

            for i in range(3):
                for l in range(LV):
                    a, b = coef(4, l, i), coef(5, l, i)
                    for q in slots:
                        here = pl.ds(at(q, l, i), 8)
                        t1[slot(q, l, i), :] = au[here, :] - a * dx[here, :] - b * dy[here, :]
            for i in range(3):
                c = [[t1[slot(q, l, i), :] for l in range(LV)] for q in slots]
                for l in range(LV):
                    cxp, cxm, cyp, cym = (coef(j, l, i) for j in range(4))
                    w = coef(6, l, i)
                    for q in slots:
                        r = tenfold(c[q], l)
                        r += cxp * t1[slot(q, l, i, 1), :] + cxm * t1[slot(q, l, i, -1), :]
                        r += cyp * right(c[q][l]) + cym * left(c[q][l])
                        t2[slot(q, l, i), :] = w * r
            for i in range(3):
                c = [[t2[slot(q, l, i), :] for l in range(LV)] for q in slots]
                for l in range(LV):
                    cxp, cxm = coef(0, l, i, -1), coef(1, l, i, 1)
                    cyp, cym = coef(2, l, i), coef(3, l, i)
                    a, b = coef(4, l, i), coef(5, l, i)
                    for q in slots:
                        r = tenfold(c[q], l)
                        r += cxm * t2[slot(q, l, i, 1), :] + cxp * t2[slot(q, l, i, -1), :]
                        r += right(cym * c[q][l]) + left(cyp * c[q][l])
                        here = pl.ds(at(q, l, i) + PAD, 8)
                        va[here, :] += r
                        pa[here, :] += a * r
                        qa[here, :] += b * r
            return 0

        lax.fori_loop(0, NP // GROUP // UNROLL, some, 0)
        return 0

    lax.fori_loop(0, got.shape[0] // (KINDS * ROWS), one_window, 0)

    def mask(f, _):
        for i in range(3):
            at = pl.ds(aligned(PAD + f * ROWS + 8 * i), 8)
            for ref in (va, pa, qa):
                ref[at, :] = jnp.where(inside[i], ref[at, :], 0.0)
        return 0

    lax.fori_loop(0, NP, mask, 0, unroll=4)
    core_lane = (lane % WIN >= MARGIN) & (lane % WIN < MARGIN + OWN)

    def last(p, _):
        for i in range(2):
            at = [aligned(PAD + (p * LV + l) * ROWS + 8 * i) + HALO for l in range(LV)]
            c = [va[pl.ds(at[l], 8), :] for l in range(LV)]
            done = []
            for l in range(LV):
                q = qa[pl.ds(at[l], 8), :]
                r = levels(c, l)
                xs = va[pl.ds(at[l] + 1, 8), :] + va[pl.ds(at[l] - 1, 8), :]
                r += 0.15 * (xs + (right(c[l]) + left(c[l])))
                r += (pa[pl.ds(at[l] + 1, 8), :] - pa[pl.ds(at[l] - 1, 8), :]) + (
                    right(q) - left(q)
                )
                done.append(jnp.where(core_lane, r, 0.0))
            for ref, values in (
                (s, swap_groups(done)),
                (om, swap_groups([u[pl.ds(at[l], 8), :] for l in range(LV)])),
            ):
                for k in range(GROUP):
                    ref[pl.ds(aligned((p * GROUP + k) * RX + 8 * i), 8), :] = values[k]
        return 0

    lax.fori_loop(0, NP // GROUP, last, 0)

    both = jnp.zeros((2 * NP, NP), F32)
    for x in range(RX):
        sx = s[pl.ds(x, NP, stride=RX), :]
        share[pl.ds(x * NP, NP), :] = sx
        rows = jnp.concatenate([sx, om[pl.ds(x, NP, stride=RX), :]], axis=0)
        both += product(rows, sx, ((1,), (1,)))
    spread = (iota((NP, LANES), 1) % NP == iota((NP, LANES), 0)).astype(F32)
    both = product(both, spread, ((1,), (0,)))
    gram, cross = both[:NP], both[NP:]
    shifted = pltpu.roll(cross, 16, 1)
    lane = iota((8, 128), 1)
    packed = jnp.zeros((8, 128), F32)
    for b in range(4):
        packed = jnp.where(lane // 32 == b, gram[8 * b : 8 * b + 8], packed)
    spare = (lane < 64) & (lane % 32 >= 16)
    for kind in range(4):
        rb, src = kind // 2, (cross if kind % 2 else shifted)
        piece = jnp.where(lane < 32, src[16 * rb : 16 * rb + 8], src[16 * rb + 8 : 16 * rb + 16])
        value = jnp.where(spare, piece, packed)
        for i in range(4):
            msg[pl.ds((4 * i + kind) * 8, 8), :] = value


def sum_kernel(parts, msg):
    n = parts.shape[0] // 8
    s = parts[pl.ds(0, 8), :]
    for g in range(1, n):
        s = s + parts[pl.ds(8 * g, 8), :]
    for d in range(msg.shape[0] // 8):
        msg[pl.ds(8 * d, 8), :] = s


def basis_kernel(parts, share, msg, *, scale):
    n = parts.shape[0] // 8
    s = parts[pl.ds(0, 8), :]
    for g in range(1, n):
        s = s + parts[pl.ds(8 * g, 8), :]
    lane8 = iota((8, 128), 1) // 32
    rows = [all_blocks(jnp.where(lane8 == b, s, 0.0)) for b in range(4)]
    gram = jnp.concatenate(rows, axis=0)
    square = jnp.concatenate([gram] * 4, axis=0)
    flipped = square.T[:NP]
    row, lane = iota((NP, 128), 0), iota((NP, 128), 1)
    a = jnp.where((row < 16) & (lane % 32 >= 16), flipped, gram)
    a = jnp.where(lane < NP, a, jnp.where(lane - NP == row, 1.0, 0.0))
    for j in range(0, NP - 2, 2):
        f0 = jnp.broadcast_to(a[:, j : j + 1], a.shape)
        f1 = jnp.broadcast_to(a[:, j + 1 : j + 2], a.shape)
        r0, r1 = a[j : j + 1], a[j + 1 : j + 2]
        p, q, r = f0[j : j + 1], f0[j + 1 : j + 2], f1[j + 1 : j + 2]
        inv = 1.0 / (p * r - q * q)
        s0, s1 = (r * r0 - q * r1) * inv, (p * r1 - q * r0) * inv
        a = a - jnp.where(row > j + 1, f0 * s0 + f1 * s1, 0.0)
    above = pltpu.roll(a, 1, 0)
    left = lane == row - 1
    p = jnp.sum(jnp.where(left, above, 0.0), axis=1, keepdims=True)
    q = jnp.sum(jnp.where(left, a, 0.0), axis=1, keepdims=True)
    a = jnp.where(row % 2 == 1, a - (q / jnp.where(p > 0.0, p, 1.0)) * above, a)
    diag = jnp.sum(jnp.where(lane == row, a, 0.0), axis=1, keepdims=True)
    inverse = jnp.where(lane // 32 == 1, a * (scale / jnp.sqrt(diag)), 0.0)
    inverse = all_blocks(inverse)
    r = iota((NP, NP), 0)
    pick = (iota((NP, NP), 1) == 2 * (r % 16) + r // 16).astype(F32)
    rows = product(pick, inverse, ((1,), (0,)))[:, :NP]
    mine = (lane[:16] % WIN >= MARGIN) & (lane[:16] % WIN < MARGIN + OWN)
    for x in range(RX):
        out = product(rows, share[pl.ds(x * NP, NP), :], ((1,), (0,)))
        both = jnp.where(mine, out[:16], pltpu.roll(out[16:], OWN, 1))
        msg[pl.ds(x, 16, stride=24), :] = both
    for d in range(16):
        msg[pl.ds(24 * d + 16, 8), :] = s


def finish_kernel(got, basis, core, *, factor):
    lane = iota((8, 128), 1)
    for xt in range(2):
        for h in range(2):
            sources = [got[pl.ds(24 * (8 * h + d) + 8 * xt, 8), :] for d in range(8)]
            for j in range(2):
                for l in range(LV):
                    acc = jnp.zeros((8, 128), F32)
                    for d in range(8):
                        shift = (OWN * d - WIN * l - MARGIN - OWN * j) % LANES
                        acc = jnp.where(lane // OWN == d, pltpu.roll(sources[d], shift, 1), acc)
                    basis[
                        pl.ds((j * LV + l) * RX + 8 * xt, 8), pl.ds(h * LANES, LANES)
                    ] = acc
    rows = []
    for rb in range(2):
        for half in range(2):
            first = 16 + 32 * half
            row = jnp.zeros((8, 128), F32)
            for cb in range(2):
                tile = got[pl.ds((3 * (2 * rb + cb) + 2) * 8, 8), :]
                moved = pltpu.roll(tile, (16 * cb - first) % 128, 1)
                row = jnp.where(lane // 16 == cb, moved, row)
            rows.append(row)
    core[...] = jnp.concatenate(rows, axis=0)[:, :NP] * factor


def shape(*dims):
    return jax.ShapeDtypeStruct(dims, F32)


def call(kernel, specs, outs, scratch=(), cost=None):
    many = isinstance(outs, tuple)
    return pl.pallas_call(
        kernel,
        out_shape=outs,
        in_specs=specs,
        out_specs=(VM,) * len(outs) if many else VM,
        scratch_shapes=list(scratch),
        cost_estimate=cost,
        compiler_params=pltpu.CompilerParams(vmem_limit_bytes=24 << 20),
    )


def on_device(probes, wind, station_cell, obs_count, obs_weight):
    tiles, groups = lax.axis_size("space"), lax.axis_size("obs")
    raw, patch, up, down = call(
        prepare_kernel,
        [VM] * 4 + [SM],
        (
            shape(KINDS * LV * RX, NY),
            shape(NP * RX, LANES),
            shape(MSG, LANES),
            shape(MSG, LANES),
        ),
    )(
        probes.reshape(NP * LV * RX, NY),
        wind.reshape(4 * LV * RX, NY),
        station_cell,
        obs_weight,
        obs_count,
    )
    low = lax.ppermute(up, "space", [(i, i + 1) for i in range(tiles - 1)])
    high = lax.ppermute(down, "space", [(i + 1, i) for i in range(tiles - 1)])
    own = call(
        own_kernel,
        [VM],
        shape(groups * KINDS * RX, LANES),
        cost=pl.CostEstimate(flops=2000000, bytes_accessed=4000000, transcendentals=0),
    )(raw)
    msg = call(
        message_kernel,
        [VM] * 3,
        shape(groups * KINDS * ROWS, LANES),
        (pltpu.VMEM((KINDS * LV, 2, 8, LANES), F32),),
    )(own, low, high)
    got = lax.all_to_all(msg.reshape(groups, KINDS * ROWS, LANES), "obs", 0, 0, tiled=True)
    field = pltpu.VMEM((NP * ROWS, LANES), F32)
    padded = pltpu.VMEM((NP * ROWS + 2 * PAD, LANES), F32)
    share, msg = call(
        patch_kernel,
        [VM] * 4,
        (shape(RX * NP, LANES), shape(groups * 8, 128)),
        (
            padded,
            field,
            field,
            field,
            pltpu.VMEM((7 * LV * SLOT, LANES), F32),
            pltpu.VMEM((UNROLL * LV * SLOT, LANES), F32),
            pltpu.VMEM((UNROLL * LV * SLOT, LANES), F32),
            padded,
            padded,
            padded,
            pltpu.VMEM((NP * RX, LANES), F32),
            pltpu.VMEM((NP * RX, LANES), F32),
        ),
    )(got.reshape(groups * KINDS * ROWS, LANES), patch, low, high)
    got = lax.all_to_all(msg.reshape(groups, 8, 128), "obs", 0, 0, tiled=True)
    msg = call(sum_kernel, [VM], shape(tiles * 8, 128))(got.reshape(groups * 8, 128))
    got = lax.all_to_all(msg.reshape(tiles, 8, 128), "space", 0, 0, tiled=True)
    scale = math.sqrt(LV * RX * tiles * NY)
    msg = call(
        lambda *refs: basis_kernel(*refs, scale=scale), [VM] * 2, shape(groups * 24, LANES)
    )(got.reshape(tiles * 8, 128), share)
    got = lax.all_to_all(msg.reshape(groups, 24, LANES), "obs", 0, 0, tiled=True)
    factor = 1.0 / (groups * tiles * station_cell.shape[1])
    basis, core = call(
        lambda *refs: finish_kernel(*refs, factor=factor),
        [VM],
        (shape(2 * LV * RX, NY), shape(NP, NP)),
    )(got.reshape(groups * 24, LANES))
    return basis.reshape(2, LV, RX, NY), core


def solution(mesh):
    in_specs = (
        P(None, None, "space", None),
        P("obs", None, None, None, "space", None),
        P("obs", "space"),
        P("obs", "space"),
        P("obs", "space"),
    )
    out_specs = (P("obs", None, "space", None), P())
    return jax.shard_map(
        on_device, mesh=mesh, in_specs=in_specs, out_specs=out_specs, check_vma=False
    )
```

```python
import math

import jax
import jax.numpy as jnp
from jax import lax
from jax.experimental import pallas as pl
from jax.experimental.pallas import tpu as pltpu
from jax.sharding import PartitionSpec as P

F32 = jnp.float32
HIGH = lax.Precision.HIGHEST
VM = pl.BlockSpec(memory_space=pltpu.VMEM)
SM = pl.BlockSpec(memory_space=pltpu.SMEM)
NT = (((1,), (1,)), ((), ()))

NP, LV, RX, NY = 32, 4, 16, 256
OWN = 16
WIN = 32
MARGIN = 8
HALO = 4
ROWS = RX + 2 * HALO
LANES = 128
GROUP = LANES // WIN
PAD = 8
UNROLL = 4
SLOT = ROWS + 2 * PAD
KINDS = 5
FIRST = (1, 1, 2, 2, 2)
COUNT = tuple(ROWS - 2 * f for f in FIRST)
START = tuple(sum(COUNT[:k]) for k in range(KINDS))
TALL = sum(COUNT)
SIDE = KINDS * LV * HALO
MSG = 2 * SIDE + NP * HALO


def iota(shape, dim):
    return lax.broadcasted_iota(jnp.int32, shape, dim)


def aligned(row):
    return pl.multiple_of(row, 8)


def live_weights(weight_ref, count_ref):
    w = weight_ref[...]
    return jnp.where(iota(w.shape, 1) < count_ref[0, 0], w, 0.0)


def weight_map(cell_row, live):
    cell = cell_row.astype(jnp.int32)
    row, col = cell // NY, cell % NY
    nslot = cell.shape[1]
    on_col = (iota((NY, nslot), 0) == col).astype(jnp.bfloat16)
    on_row = iota((LV * RX, nslot), 0) == row
    total = jnp.zeros((LV * RX, NY), F32)
    rest = live
    for _ in range(3):
        part = rest.astype(jnp.bfloat16).astype(F32)
        rest = rest - part
        lhs = jnp.where(on_row, part, 0.0).astype(jnp.bfloat16)
        total += lax.dot_general(lhs, on_col, NT, preferred_element_type=F32)
    return total


def window(tiles, first):
    shape = tiles[0][0].shape
    lane = iota(shape, 1)
    col = first + lane % WIN
    acc = None
    for k, (lo, hi) in enumerate(tiles):
        if isinstance(first, int) and first + WIN <= LANES:
            both = lo
        elif isinstance(first, int) and first >= LANES:
            both = hi
        else:
            both = jnp.where((lane >= first) & (lane < first + WIN), lo, hi)
        shift = k * WIN - first + 2 * LANES
        shift = shift % LANES if isinstance(first, int) else lax.rem(shift, LANES)
        both = pltpu.roll(both, shift, 1)
        acc = both if acc is None else jnp.where(lane // WIN == k, both, acc)
    return jnp.where((col >= 0) & (col < NY), acc, 0.0)


def prepare_kernel(
    probes_far, wind_far, cells_far, weight_far, count, raw, patch, up, down,
    probes, wind, cells, weight, sems,
):
    copies = [
        pltpu.make_async_copy(far, near, sems.at[i])
        for i, (far, near) in enumerate(
            (
                (cells_far, cells),
                (weight_far, weight),
                (wind_far, wind),
                (probes_far, probes),
            )
        )
    ]
    for copy in copies:
        copy.start()
    first = lax.axis_index("obs") * OWN - MARGIN
    copies[0].wait()
    copies[1].wait()
    copies[2].wait()
    for i in range(4 * LV):
        raw[pl.ds(i * RX, RX), :] = 0.5 * wind[pl.ds(i * RX, RX), :]
    raw[pl.ds(4 * LV * RX, LV * RX), :] = weight_map(
        cells[...].astype(F32), live_weights(weight, count)
    )

    copies[3].wait()

    def one(p, _):
        for l in range(LV):
            for xt in range(2):
                tiles = [
                    [
                        probes[
                            pl.ds(aligned(((p * GROUP + k) * LV + l) * RX + 8 * xt), 8),
                            pl.ds(h * LANES, LANES),
                        ]
                        for h in range(2)
                    ]
                    for k in range(GROUP)
                ]
                patch[pl.ds(aligned((p * LV + l) * RX + 8 * xt), 8), :] = window(tiles, first)
        return 0

    lax.fori_loop(0, NP // GROUP, one, 0)
    for out, start in ((up, RX - HALO), (down, 0)):
        for h in range(2):
            for i in range(KINDS * LV):
                out[pl.ds(h * SIDE + i * HALO, HALO), :] = raw[
                    pl.ds(i * RX + start, HALO), pl.ds(h * LANES, LANES)
                ]
        for p in range(NP):
            out[pl.ds(2 * SIDE + p * HALO, HALO), :] = patch[pl.ds(p * RX + start, HALO), :]


def own_kernel(raw, own):
    for kind in range(KINDS):
        for xt in range(2):
            tiles = [
                [
                    raw[pl.ds((kind * LV + l) * RX + 8 * xt, 8), pl.ds(h * LANES, LANES)]
                    for h in range(2)
                ]
                for l in range(LV)
            ]
            for d in range(NY // OWN):
                own[pl.ds((d * KINDS + kind) * RX + 8 * xt, 8), :] = window(
                    tiles, d * OWN - MARGIN
                )


def message_kernel(own, low, high, msg, edge):
    for h in range(2):
        for i in range(KINDS * LV):
            src = pl.ds(h * SIDE + i * HALO, HALO)
            edge[i, h, pl.ds(0, HALO), :] = low[src, :]
            edge[i, h, pl.ds(HALO, HALO), :] = high[src, :]
    for kind in range(KINDS):
        tiles = [[edge[kind * LV + l, h] for h in range(2)] for l in range(LV)]
        for d in range(NY // OWN):
            value = window(tiles, d * OWN - MARGIN)
            base, n = d * TALL + START[kind], HALO - FIRST[kind]
            msg[pl.ds(base, n), :] = value[HALO - n : HALO]
            msg[pl.ds(base + n, RX), :] = own[pl.ds((d * KINDS + kind) * RX, RX), :]
            msg[pl.ds(base + n + RX, n), :] = value[HALO : HALO + n]


def all_blocks(t):
    return t + pltpu.roll(t, 32, 1) + pltpu.roll(t, 64, 1) + pltpu.roll(t, 96, 1)


def product(a, b, dims):
    return lax.dot_general(a, b, (dims, ((), ())), precision=HIGH, preferred_element_type=F32)


def level_sum(c, l):
    if l == 0:
        return c[1]
    if l == LV - 1:
        return c[l - 1]
    return c[l - 1] + c[l + 1]


def swap_groups(v):
    lane = iota(v[0].shape, 1)
    low, even = lane < 64, lane // 32 % 2 == 0

    def half(w):
        return pltpu.roll(w, 64, 1)

    x = [
        jnp.where(low, v[0], half(v[2])),
        jnp.where(low, v[1], half(v[3])),
        jnp.where(low, half(v[0]), v[2]),
        jnp.where(low, half(v[1]), v[3]),
    ]
    out = []
    for a in (0, 2):
        out.append(jnp.where(even, x[a], pltpu.roll(x[a + 1], 32, 1)))
        out.append(jnp.where(even, pltpu.roll(x[a], 96, 1), x[a + 1]))
    return out


def patch_kernel(
    got, patch, low, high, share, msg, u, au, dx, dy, cf, t1, t2, va, pa, qa, s, om
):
    t, o = lax.axis_index("space"), lax.axis_index("obs")
    tiles = lax.axis_size("space")
    lane = iota((8, LANES), 1)
    col = o * OWN - MARGIN + lane % WIN
    inside = []
    for i in range(3):
        row = t * RX - HALO + 8 * i + iota((8, LANES), 0)
        inside.append((row >= 0) & (row < tiles * RX) & (col >= 0) & (col < NY))

    def right(c):
        return pltpu.roll(c, LANES - 1, 1)

    def left(c):
        return pltpu.roll(c, 1, 1)

    def levels(c, l):
        return 0.2 * c[l] + 0.1 * level_sum(c, l)

    def tenfold(c, l):
        return (c[l] + c[l]) + level_sum(c, l)

    edge = jnp.zeros((PAD, LANES), F32)
    for ref in (u, va, pa, qa):
        ref[pl.ds(0, PAD), :] = edge
        ref[pl.ds(PAD + NP * ROWS, PAD), :] = edge
    cf[...] = jnp.zeros(cf.shape, F32)
    for ref, n in ((t1, UNROLL * LV), (t2, UNROLL * LV)):
        for j in range(n):
            ref[pl.ds(j * SLOT, PAD), :] = edge
            ref[pl.ds(j * SLOT + PAD + ROWS, PAD), :] = edge
    for f in range(NP):
        base = PAD + f * ROWS
        u[pl.ds(base, HALO), :] = low[pl.ds(2 * SIDE + f * HALO, HALO), :]
        u[pl.ds(base + HALO, RX), :] = patch[pl.ds(f * RX, RX), :]
        u[pl.ds(base + HALO + RX, HALO), :] = high[pl.ds(2 * SIDE + f * HALO, HALO), :]

    def shared(p, _):
        for i in range(3):
            at = [aligned((p * LV + l) * ROWS + 8 * i) for l in range(LV)]
            c = [u[pl.ds(at[l] + PAD, 8), :] for l in range(LV)]
            for l in range(LV):
                xp, xm = u[pl.ds(at[l] + PAD + 1, 8), :], u[pl.ds(at[l] + PAD - 1, 8), :]
                yp, ym = right(c[l]), left(c[l])
                mean = 0.01 * tenfold(c, l) + 0.015 * ((xp + xm) + (yp + ym))
                here = pl.ds(at[l], 8)
                au[here, :] = jnp.where(inside[i], mean, 0.0)
                dx[here, :] = jnp.where(inside[i], 0.1 * (xp - xm), 0.0)
                dy[here, :] = jnp.where(inside[i], 0.1 * (yp - ym), 0.0)
                for ref in (va, pa, qa):
                    ref[pl.ds(at[l] + PAD, 8), :] = edge
        return 0

    lax.fori_loop(0, NP // GROUP, shared, 0)

    def coef(j, l, i, off=0):
        return cf[pl.ds((j * LV + l) * SLOT + PAD + 8 * i + off, 8), :]

    def one_window(g, _):
        base = g * TALL
        for kind in range(KINDS):
            for off in (0, 8, COUNT[kind] - 8):
                tile = got[pl.ds(base + START[kind] + off, 8), :]
                row = PAD + FIRST[kind] + off
                for l in range(LV):
                    m = jnp.take_along_axis(tile, l * WIN + lane % WIN, axis=1)
                    if kind in (2, 3):
                        m = 10.0 * m
                        pair = ((2 * kind - 4, 1.5 - m), (2 * kind - 3, 1.5 + m))
                    else:
                        pair = (({0: 4, 1: 5, 4: 6}[kind], 0.1 * m if kind == 4 else m),)
                    for j, value in pair:
                        cf[pl.ds((j * LV + l) * SLOT + row, 8), :] = value

        def some(step, _):
            slots = range(UNROLL)

            def at(q, l, i):
                return aligned(((step * UNROLL + q) * LV + l) * ROWS + 8 * i)

            def slot(q, l, i, off=0):
                return pl.ds((q * LV + l) * SLOT + PAD + 8 * i + off, 8)

            for i in range(3):
                for l in range(LV):
                    a, b = coef(4, l, i), coef(5, l, i)
                    for q in slots:
                        here = pl.ds(at(q, l, i), 8)
                        t1[slot(q, l, i), :] = au[here, :] - a * dx[here, :] - b * dy[here, :]
            for i in range(3):
                c = [[t1[slot(q, l, i), :] for l in range(LV)] for q in slots]
                for l in range(LV):
                    cxp, cxm, cyp, cym = (coef(j, l, i) for j in range(4))
                    w = coef(6, l, i)
                    for q in slots:
                        r = tenfold(c[q], l)
                        r += cxp * t1[slot(q, l, i, 1), :] + cxm * t1[slot(q, l, i, -1), :]
                        r += cyp * right(c[q][l]) + cym * left(c[q][l])
                        t2[slot(q, l, i), :] = w * r
            for i in range(3):
                c = [[t2[slot(q, l, i), :] for l in range(LV)] for q in slots]
                for l in range(LV):
                    cxp, cxm = coef(0, l, i, -1), coef(1, l, i, 1)
                    cyp, cym = coef(2, l, i), coef(3, l, i)
                    a, b = coef(4, l, i), coef(5, l, i)
                    for q in slots:
                        r = tenfold(c[q], l)
                        r += cxm * t2[slot(q, l, i, 1), :] + cxp * t2[slot(q, l, i, -1), :]
                        r += right(cym * c[q][l]) + left(cyp * c[q][l])
                        here = pl.ds(at(q, l, i) + PAD, 8)
                        va[here, :] += r
                        pa[here, :] += a * r
                        qa[here, :] += b * r
            return 0

        lax.fori_loop(0, NP // GROUP // UNROLL, some, 0)
        return 0

    lax.fori_loop(0, got.shape[0] // TALL, one_window, 0)

    def mask(f, _):
        for i in range(3):
            at = pl.ds(aligned(PAD + f * ROWS + 8 * i), 8)
            for ref in (va, pa, qa):
                ref[at, :] = jnp.where(inside[i], ref[at, :], 0.0)
        return 0

    lax.fori_loop(0, NP, mask, 0, unroll=4)
    core_lane = (lane % WIN >= MARGIN) & (lane % WIN < MARGIN + OWN)

    def last(p, _):
        tiles_of = []
        for i in range(2):
            at = [aligned(PAD + (p * LV + l) * ROWS + 8 * i) + HALO for l in range(LV)]
            c = [va[pl.ds(at[l], 8), :] for l in range(LV)]
            done = []
            for l in range(LV):
                q = qa[pl.ds(at[l], 8), :]
                r = levels(c, l)
                xs = va[pl.ds(at[l] + 1, 8), :] + va[pl.ds(at[l] - 1, 8), :]
                r += 0.15 * (xs + (right(c[l]) + left(c[l])))
                r += (pa[pl.ds(at[l] + 1, 8), :] - pa[pl.ds(at[l] - 1, 8), :]) + (
                    right(q) - left(q)
                )
                done.append(jnp.where(core_lane, r, 0.0))
            own = [jnp.where(core_lane, u[pl.ds(at[l], 8), :], 0.0) for l in range(LV)]
            tiles_of.append((swap_groups(done), swap_groups(own)))
        for n, ref in enumerate((s, om)):
            for k in range(GROUP):
                first, second = tiles_of[0][n][k], tiles_of[1][n][k]
                ref[pl.ds(aligned((p * GROUP + k) * 8), 8), :] = first + pltpu.roll(second, OWN, 1)
        return 0

    lax.fori_loop(0, NP // GROUP, last, 0)

    both = jnp.zeros((2 * NP, NP), F32)
    for x in range(8):
        sx = s[pl.ds(x, NP, stride=8), :]
        share[pl.ds(x * NP, NP), :] = sx
        rows = jnp.concatenate([sx, om[pl.ds(x, NP, stride=8), :]], axis=0)
        both += product(rows, sx, ((1,), (1,)))
    spread = (iota((NP, LANES), 1) % NP == iota((NP, LANES), 0)).astype(F32)
    both = product(both, spread, ((1,), (0,)))
    gram, cross = both[:NP], both[NP:]
    shifted = pltpu.roll(cross, 16, 1)
    lane = iota((8, 128), 1)
    packed = jnp.zeros((8, 128), F32)
    for b in range(4):
        packed = jnp.where(lane // 32 == b, gram[8 * b : 8 * b + 8], packed)
    spare = (lane < 64) & (lane % 32 >= 16)
    for kind in range(4):
        rb, src = kind // 2, (cross if kind % 2 else shifted)
        piece = jnp.where(lane < 32, src[16 * rb : 16 * rb + 8], src[16 * rb + 8 : 16 * rb + 16])
        value = jnp.where(spare, piece, packed)
        for i in range(4):
            msg[pl.ds((4 * i + kind) * 8, 8), :] = value


def sum_kernel(parts, msg):
    n = parts.shape[0] // 8
    s = parts[pl.ds(0, 8), :]
    for g in range(1, n):
        s = s + parts[pl.ds(8 * g, 8), :]
    for d in range(msg.shape[0] // 8):
        msg[pl.ds(8 * d, 8), :] = s


def basis_kernel(parts, share, msg, *, scale):
    n = parts.shape[0] // 8
    s = parts[pl.ds(0, 8), :]
    for g in range(1, n):
        s = s + parts[pl.ds(8 * g, 8), :]
    lane8 = iota((8, 128), 1) // 32
    rows = [all_blocks(jnp.where(lane8 == b, s, 0.0)) for b in range(4)]
    gram = jnp.concatenate(rows, axis=0)
    square = jnp.concatenate([gram] * 4, axis=0)
    flipped = square.T[:NP]
    row, lane = iota((NP, 128), 0), iota((NP, 128), 1)
    a = jnp.where((row < 16) & (lane % 32 >= 16), flipped, gram)
    a = jnp.where(lane < NP, a, jnp.where(lane - NP == row, 1.0, 0.0))
    for j in range(0, NP - 2, 2):
        f0 = jnp.broadcast_to(a[:, j : j + 1], a.shape)
        f1 = jnp.broadcast_to(a[:, j + 1 : j + 2], a.shape)
        r0, r1 = a[j : j + 1], a[j + 1 : j + 2]
        p, q, r = f0[j : j + 1], f0[j + 1 : j + 2], f1[j + 1 : j + 2]
        inv = 1.0 / (p * r - q * q)
        s0, s1 = (r * r0 - q * r1) * inv, (p * r1 - q * r0) * inv
        a = a - jnp.where(row > j + 1, f0 * s0 + f1 * s1, 0.0)
    above = pltpu.roll(a, 1, 0)
    left = lane == row - 1
    p = jnp.sum(jnp.where(left, above, 0.0), axis=1, keepdims=True)
    q = jnp.sum(jnp.where(left, a, 0.0), axis=1, keepdims=True)
    a = jnp.where(row % 2 == 1, a - (q / jnp.where(p > 0.0, p, 1.0)) * above, a)
    diag = jnp.sum(jnp.where(lane == row, a, 0.0), axis=1, keepdims=True)
    inverse = jnp.where(lane // 32 == 1, a * (scale / jnp.sqrt(diag)), 0.0)
    inverse = all_blocks(inverse)
    r = iota((NP, NP), 0)
    pick = (iota((NP, NP), 1) == 2 * (r % 16) + r // 16).astype(F32)
    rows = product(pick, inverse, ((1,), (0,)))[:, :NP]
    for x in range(8):
        out = product(rows, share[pl.ds(x * NP, NP), :], ((1,), (0,)))
        for j in range(2):
            msg[pl.ds(8 * j + x, 16, stride=24), :] = out[16 * j : 16 * j + 16]
    for d in range(16):
        msg[pl.ds(24 * d + 16, 8), :] = s


def finish_kernel(got, basis, core, *, factor):
    lane = iota((8, 128), 1)
    for j in range(2):
        for h in range(2):
            sources = [got[pl.ds(24 * (8 * h + d) + 8 * j, 8), :] for d in range(8)]
            for xt in range(2):
                for l in range(LV):
                    acc = jnp.zeros((8, 128), F32)
                    for d in range(8):
                        shift = (OWN * d - WIN * l - MARGIN - OWN * xt) % LANES
                        acc = jnp.where(lane // OWN == d, pltpu.roll(sources[d], shift, 1), acc)
                    basis[
                        pl.ds((j * LV + l) * RX + 8 * xt, 8), pl.ds(h * LANES, LANES)
                    ] = acc
    rows = []
    for rb in range(2):
        for half in range(2):
            first = 16 + 32 * half
            row = jnp.zeros((8, 128), F32)
            for cb in range(2):
                tile = got[pl.ds((3 * (2 * rb + cb) + 2) * 8, 8), :]
                moved = pltpu.roll(tile, (16 * cb - first) % 128, 1)
                row = jnp.where(lane // 16 == cb, moved, row)
            rows.append(row)
    core[...] = jnp.concatenate(rows, axis=0)[:, :NP] * factor


def shape(*dims):
    return jax.ShapeDtypeStruct(dims, F32)


def call(kernel, specs, outs, scratch=(), cost=None, grant=24 << 20):
    many = isinstance(outs, tuple)
    return pl.pallas_call(
        kernel,
        out_shape=outs,
        in_specs=specs,
        out_specs=(VM,) * len(outs) if many else VM,
        scratch_shapes=list(scratch),
        cost_estimate=cost,
        compiler_params=pltpu.CompilerParams(
            vmem_limit_bytes=grant
        ),
    )


def on_device(probes, wind, station_cell, obs_count, obs_weight):
    tiles, groups = lax.axis_size("space"), lax.axis_size("obs")
    raw, patch, up, down = call(
        prepare_kernel,
        [pl.BlockSpec(memory_space=pltpu.HBM)] * 4 + [SM],
        (
            shape(KINDS * LV * RX, NY),
            shape(NP * RX, LANES),
            shape(MSG, LANES),
            shape(MSG, LANES),
        ),
        (
            pltpu.VMEM((NP * LV * RX, NY), F32),
            pltpu.VMEM((4 * LV * RX, NY), F32),
            pltpu.VMEM(station_cell.shape, jnp.int32),
            pltpu.VMEM(obs_weight.shape, F32),
            pltpu.SemaphoreType.DMA((4,)),
        ),
        grant=60 * 1024 * 1024,
    )(
        probes.reshape(NP * LV * RX, NY),
        wind.reshape(4 * LV * RX, NY),
        station_cell,
        obs_weight,
        obs_count,
    )
    low = lax.ppermute(up, "space", [(i, i + 1) for i in range(tiles - 1)])
    high = lax.ppermute(down, "space", [(i + 1, i) for i in range(tiles - 1)])
    own = call(
        own_kernel,
        [VM],
        shape(groups * KINDS * RX, LANES),
        cost=pl.CostEstimate(flops=2000000, bytes_accessed=4000000, transcendentals=0),
    )(raw)
    msg = call(
        message_kernel,
        [VM] * 3,
        shape(groups * TALL, LANES),
        (pltpu.VMEM((KINDS * LV, 2, 8, LANES), F32),),
    )(own, low, high)
    got = lax.all_to_all(msg.reshape(groups, TALL, LANES), "obs", 0, 0, tiled=True)
    field = pltpu.VMEM((NP * ROWS, LANES), F32)
    padded = pltpu.VMEM((NP * ROWS + 2 * PAD, LANES), F32)
    share, msg = call(
        patch_kernel,
        [VM] * 4,
        (shape(8 * NP, LANES), shape(groups * 8, 128)),
        (
            padded,
            field,
            field,
            field,
            pltpu.VMEM((7 * LV * SLOT, LANES), F32),
            pltpu.VMEM((UNROLL * LV * SLOT, LANES), F32),
            pltpu.VMEM((UNROLL * LV * SLOT, LANES), F32),
            padded,
            padded,
            padded,
            pltpu.VMEM((NP * 8, LANES), F32),
            pltpu.VMEM((NP * 8, LANES), F32),
        ),
    )(got.reshape(groups * TALL, LANES), patch, low, high)
    got = lax.all_to_all(msg.reshape(groups, 8, 128), "obs", 0, 0, tiled=True)
    msg = call(sum_kernel, [VM], shape(tiles * 8, 128))(got.reshape(groups * 8, 128))
    got = lax.all_to_all(msg.reshape(tiles, 8, 128), "space", 0, 0, tiled=True)
    scale = math.sqrt(LV * RX * tiles * NY)
    msg = call(
        lambda *refs: basis_kernel(*refs, scale=scale), [VM] * 2, shape(groups * 24, LANES)
    )(got.reshape(tiles * 8, 128), share)
    got = lax.all_to_all(msg.reshape(groups, 24, LANES), "obs", 0, 0, tiled=True)
    factor = 1.0 / (groups * tiles * station_cell.shape[1])
    basis, core = call(
        lambda *refs: finish_kernel(*refs, factor=factor),
        [VM],
        (shape(2 * LV * RX, NY), shape(NP, NP)),
    )(got.reshape(groups * 24, LANES))
    return basis.reshape(2, LV, RX, NY), core


def solution(mesh):
    in_specs = (
        P(None, None, "space", None),
        P("obs", None, None, None, "space", None),
        P("obs", "space"),
        P("obs", "space"),
        P("obs", "space"),
    )
    out_specs = (P("obs", None, "space", None), P())
    return jax.shard_map(
        on_device, mesh=mesh, in_specs=in_specs, out_specs=out_specs, check_vma=False
    )
```

```python
import math

import jax
import jax.numpy as jnp
from jax import lax
from jax.experimental import pallas as pl
from jax.experimental.pallas import tpu as pltpu
from jax.sharding import PartitionSpec as P

F32 = jnp.float32
HIGH = lax.Precision.HIGHEST
VM = pl.BlockSpec(memory_space=pltpu.VMEM)
SM = pl.BlockSpec(memory_space=pltpu.SMEM)
NT = (((1,), (1,)), ((), ()))

NP, LV, RX, NY = 32, 4, 16, 256
OWN = 16
WIN = 32
MARGIN = 8
HALO = 4
ROWS = RX + 2 * HALO
LANES = 128
GROUP = LANES // WIN
PAD = 8
UNROLL = 8
SLOT = ROWS + 2 * PAD
KINDS = 5
FIRST = (1, 1, 2, 2, 2)
COUNT = tuple(ROWS - 2 * f for f in FIRST)
START = tuple(sum(COUNT[:k]) for k in range(KINDS))
TALL = sum(COUNT)
CHUNK = NP * LV * RX // 4
SIDE = KINDS * LV * HALO
MSG = 2 * SIDE + NP * HALO


def iota(shape, dim):
    return lax.broadcasted_iota(jnp.int32, shape, dim)


def aligned(row):
    return pl.multiple_of(row, 8)


def live_weights(weight_ref, count_ref):
    w = weight_ref[...]
    return jnp.where(iota(w.shape, 1) < count_ref[0, 0], w, 0.0)


def weight_map(cell_row, live):
    cell = cell_row.astype(jnp.int32)
    row, col = cell // NY, cell % NY
    nslot = cell.shape[1]
    on_col = (iota((NY, nslot), 0) == col).astype(jnp.bfloat16)
    on_row = iota((LV * RX, nslot), 0) == row
    total = jnp.zeros((LV * RX, NY), F32)
    rest = live
    for _ in range(3):
        part = rest.astype(jnp.bfloat16).astype(F32)
        rest = rest - part
        lhs = jnp.where(on_row, part, 0.0).astype(jnp.bfloat16)
        total += lax.dot_general(lhs, on_col, NT, preferred_element_type=F32)
    return total


def window(tiles, first):
    shape = tiles[0][0].shape
    lane = iota(shape, 1)
    col = first + lane % WIN
    acc = None
    for k, (lo, hi) in enumerate(tiles):
        if isinstance(first, int) and first + WIN <= LANES:
            both = lo
        elif isinstance(first, int) and first >= LANES:
            both = hi
        else:
            both = jnp.where((lane >= first) & (lane < first + WIN), lo, hi)
        shift = k * WIN - first + 2 * LANES
        shift = shift % LANES if isinstance(first, int) else lax.rem(shift, LANES)
        both = pltpu.roll(both, shift, 1)
        acc = both if acc is None else jnp.where(lane // WIN == k, both, acc)
    return jnp.where((col >= 0) & (col < NY), acc, 0.0)


def prepare_kernel(
    probes_far, wind_far, cells_far, weight_far, count, raw, patch, up, down,
    probes, wind, cells, weight, sems,
):
    copies = [
        pltpu.make_async_copy(far, near, sems.at[i])
        for i, (far, near) in enumerate(
            (
                (cells_far, cells),
                (weight_far, weight),
                (wind_far, wind),
                *(
                    (probes_far.at[pl.ds(c * CHUNK, CHUNK), :], probes.at[pl.ds(c * CHUNK, CHUNK), :])
                    for c in range(4)
                ),
            )
        )
    ]
    for copy in copies:
        copy.start()
    first = lax.axis_index("obs") * OWN - MARGIN
    copies[0].wait()
    copies[1].wait()
    copies[2].wait()
    for i in range(4 * LV):
        raw[pl.ds(i * RX, RX), :] = 0.5 * wind[pl.ds(i * RX, RX), :]
    raw[pl.ds(4 * LV * RX, LV * RX), :] = weight_map(
        cells[...].astype(F32), live_weights(weight, count)
    )

    def one(p, _):
        for l in range(LV):
            for xt in range(2):
                tiles = [
                    [
                        probes[
                            pl.ds(aligned(((p * GROUP + k) * LV + l) * RX + 8 * xt), 8),
                            pl.ds(h * LANES, LANES),
                        ]
                        for h in range(2)
                    ]
                    for k in range(GROUP)
                ]
                patch[pl.ds(aligned((p * LV + l) * RX + 8 * xt), 8), :] = window(tiles, first)
        return 0

    for c in range(4):
        copies[3 + c].wait()
        lax.fori_loop(2 * c, 2 * c + 2, one, 0)
    for out, start in ((up, RX - HALO), (down, 0)):
        for h in range(2):
            for i in range(KINDS * LV):
                out[pl.ds(h * SIDE + i * HALO, HALO), :] = raw[
                    pl.ds(i * RX + start, HALO), pl.ds(h * LANES, LANES)
                ]
        for p in range(NP):
            out[pl.ds(2 * SIDE + p * HALO, HALO), :] = patch[pl.ds(p * RX + start, HALO), :]


def own_kernel(raw, own):
    for kind in range(KINDS):
        for xt in range(2):
            tiles = [
                [
                    raw[pl.ds((kind * LV + l) * RX + 8 * xt, 8), pl.ds(h * LANES, LANES)]
                    for h in range(2)
                ]
                for l in range(LV)
            ]
            for d in range(NY // OWN):
                own[pl.ds((d * KINDS + kind) * RX + 8 * xt, 8), :] = window(
                    tiles, d * OWN - MARGIN
                )


def message_kernel(own, low, high, msg, edge):
    for h in range(2):
        for i in range(KINDS * LV):
            src = pl.ds(h * SIDE + i * HALO, HALO)
            edge[i, h, pl.ds(0, HALO), :] = low[src, :]
            edge[i, h, pl.ds(HALO, HALO), :] = high[src, :]
    for kind in range(KINDS):
        tiles = [[edge[kind * LV + l, h] for h in range(2)] for l in range(LV)]
        for d in range(NY // OWN):
            value = window(tiles, d * OWN - MARGIN)
            base, n = d * TALL + START[kind], HALO - FIRST[kind]
            msg[pl.ds(base, n), :] = value[HALO - n : HALO]
            msg[pl.ds(base + n, RX), :] = own[pl.ds((d * KINDS + kind) * RX, RX), :]
            msg[pl.ds(base + n + RX, n), :] = value[HALO : HALO + n]


def all_blocks(t):
    return t + pltpu.roll(t, 32, 1) + pltpu.roll(t, 64, 1) + pltpu.roll(t, 96, 1)


def product(a, b, dims):
    return lax.dot_general(a, b, (dims, ((), ())), precision=HIGH, preferred_element_type=F32)


def level_sum(c, l):
    if l == 0:
        return c[1]
    if l == LV - 1:
        return c[l - 1]
    return c[l - 1] + c[l + 1]


def swap_groups(v):
    lane = iota(v[0].shape, 1)
    low, even = lane < 64, lane // 32 % 2 == 0

    def half(w):
        return pltpu.roll(w, 64, 1)

    x = [
        jnp.where(low, v[0], half(v[2])),
        jnp.where(low, v[1], half(v[3])),
        jnp.where(low, half(v[0]), v[2]),
        jnp.where(low, half(v[1]), v[3]),
    ]
    out = []
    for a in (0, 2):
        out.append(jnp.where(even, x[a], pltpu.roll(x[a + 1], 32, 1)))
        out.append(jnp.where(even, pltpu.roll(x[a], 96, 1), x[a + 1]))
    return out


def patch_kernel(
    got, patch, low, high, share, msg, u, au, dx, dy, cf, t1, t2, va, pa, qa, s, om
):
    t, o = lax.axis_index("space"), lax.axis_index("obs")
    tiles = lax.axis_size("space")
    lane = iota((8, LANES), 1)
    col = o * OWN - MARGIN + lane % WIN
    inside = []
    for i in range(3):
        row = t * RX - HALO + 8 * i + iota((8, LANES), 0)
        inside.append((row >= 0) & (row < tiles * RX) & (col >= 0) & (col < NY))

    def right(c):
        return pltpu.roll(c, LANES - 1, 1)

    def left(c):
        return pltpu.roll(c, 1, 1)

    def levels(c, l):
        return 0.2 * c[l] + 0.1 * level_sum(c, l)

    def tenfold(c, l):
        return (c[l] + c[l]) + level_sum(c, l)

    edge = jnp.zeros((PAD, LANES), F32)
    for ref in (u, va, pa, qa):
        ref[pl.ds(0, PAD), :] = edge
        ref[pl.ds(PAD + NP * ROWS, PAD), :] = edge
    cf[...] = jnp.zeros(cf.shape, F32)
    for ref, n in ((t1, UNROLL * LV), (t2, UNROLL * LV)):
        for j in range(n):
            ref[pl.ds(j * SLOT, PAD), :] = edge
            ref[pl.ds(j * SLOT + PAD + ROWS, PAD), :] = edge
    for f in range(NP):
        base = PAD + f * ROWS
        u[pl.ds(base, HALO), :] = low[pl.ds(2 * SIDE + f * HALO, HALO), :]
        u[pl.ds(base + HALO, RX), :] = patch[pl.ds(f * RX, RX), :]
        u[pl.ds(base + HALO + RX, HALO), :] = high[pl.ds(2 * SIDE + f * HALO, HALO), :]

    def shared(p, _):
        for i in range(3):
            at = [aligned((p * LV + l) * ROWS + 8 * i) for l in range(LV)]
            c = [u[pl.ds(at[l] + PAD, 8), :] for l in range(LV)]
            for l in range(LV):
                xp, xm = u[pl.ds(at[l] + PAD + 1, 8), :], u[pl.ds(at[l] + PAD - 1, 8), :]
                yp, ym = right(c[l]), left(c[l])
                mean = 0.01 * tenfold(c, l) + 0.015 * ((xp + xm) + (yp + ym))
                here = pl.ds(at[l], 8)
                au[here, :] = jnp.where(inside[i], mean, 0.0)
                dx[here, :] = jnp.where(inside[i], 0.1 * (xp - xm), 0.0)
                dy[here, :] = jnp.where(inside[i], 0.1 * (yp - ym), 0.0)
                for ref in (va, pa, qa):
                    ref[pl.ds(at[l] + PAD, 8), :] = edge
        return 0

    lax.fori_loop(0, NP // GROUP, shared, 0)

    def place(turn, j, l):
        return ((turn * 7 + j) * LV + l) * SLOT

    def expand(g, turn):
        base = g * TALL
        for kind in range(KINDS):
            for off in (0, 8, COUNT[kind] - 8):
                tile = got[pl.ds(base + START[kind] + off, 8), :]
                row = PAD + FIRST[kind] + off
                for l in range(LV):
                    m = jnp.take_along_axis(tile, l * WIN + lane % WIN, axis=1)
                    if kind in (2, 3):
                        m = 10.0 * m
                        pair = ((2 * kind - 4, 1.5 - m), (2 * kind - 3, 1.5 + m))
                    else:
                        pair = (({0: 4, 1: 5, 4: 6}[kind], 0.1 * m if kind == 4 else m),)
                    for j, value in pair:
                        cf[pl.ds(place(turn, j, l) + row, 8), :] = value

    def steps(turn):
        def coef(j, l, i, off=0):
            return cf[pl.ds(place(turn, j, l) + PAD + 8 * i + off, 8), :]

        def some(step, _):
            slots = range(UNROLL)

            def at(q, l, i):
                return aligned(((step * UNROLL + q) * LV + l) * ROWS + 8 * i)

            def slot(q, l, i, off=0):
                return pl.ds((q * LV + l) * SLOT + PAD + 8 * i + off, 8)

            for i in range(3):
                for l in range(LV):
                    a, b = coef(4, l, i), coef(5, l, i)
                    for q in slots:
                        here = pl.ds(at(q, l, i), 8)
                        t1[slot(q, l, i), :] = au[here, :] - a * dx[here, :] - b * dy[here, :]
            for i in range(3):
                c = [[t1[slot(q, l, i), :] for l in range(LV)] for q in slots]
                for l in range(LV):
                    cxp, cxm, cyp, cym = (coef(j, l, i) for j in range(4))
                    w = coef(6, l, i)
                    for q in slots:
                        r = tenfold(c[q], l)
                        r += cxp * t1[slot(q, l, i, 1), :] + cxm * t1[slot(q, l, i, -1), :]
                        r += cyp * right(c[q][l]) + cym * left(c[q][l])
                        t2[slot(q, l, i), :] = w * r
            for i in range(3):
                c = [[t2[slot(q, l, i), :] for l in range(LV)] for q in slots]
                for l in range(LV):
                    cxp, cxm = coef(0, l, i, -1), coef(1, l, i, 1)
                    cyp, cym = coef(2, l, i), coef(3, l, i)
                    a, b = coef(4, l, i), coef(5, l, i)
                    for q in slots:
                        r = tenfold(c[q], l)
                        r += cxm * t2[slot(q, l, i, 1), :] + cxp * t2[slot(q, l, i, -1), :]
                        r += right(cym * c[q][l]) + left(cyp * c[q][l])
                        here = pl.ds(at(q, l, i) + PAD, 8)
                        va[here, :] += r
                        pa[here, :] += a * r
                        qa[here, :] += b * r
            return 0

        if UNROLL == NP // GROUP:
            some(0, 0)
        else:
            lax.fori_loop(0, NP // GROUP // UNROLL, some, 0)

    windows = got.shape[0] // TALL
    expand(0, 0)

    def two_windows(h, _):
        expand(2 * h + 1, 1)
        steps(0)
        expand(jnp.minimum(2 * h + 2, windows - 1), 0)
        steps(1)
        return 0

    lax.fori_loop(0, windows // 2, two_windows, 0)

    def mask(f, _):
        for i in range(3):
            at = pl.ds(aligned(PAD + f * ROWS + 8 * i), 8)
            for ref in (va, pa, qa):
                ref[at, :] = jnp.where(inside[i], ref[at, :], 0.0)
        return 0

    lax.fori_loop(0, NP, mask, 0, unroll=4)
    core_lane = (lane % WIN >= MARGIN) & (lane % WIN < MARGIN + OWN)

    def last(p, _):
        tiles_of = []
        for i in range(2):
            at = [aligned(PAD + (p * LV + l) * ROWS + 8 * i) + HALO for l in range(LV)]
            c = [va[pl.ds(at[l], 8), :] for l in range(LV)]
            done = []
            for l in range(LV):
                q = qa[pl.ds(at[l], 8), :]
                r = levels(c, l)
                xs = va[pl.ds(at[l] + 1, 8), :] + va[pl.ds(at[l] - 1, 8), :]
                r += 0.15 * (xs + (right(c[l]) + left(c[l])))
                r += (pa[pl.ds(at[l] + 1, 8), :] - pa[pl.ds(at[l] - 1, 8), :]) + (
                    right(q) - left(q)
                )
                done.append(jnp.where(core_lane, r, 0.0))
            own = [jnp.where(core_lane, u[pl.ds(at[l], 8), :], 0.0) for l in range(LV)]
            tiles_of.append((swap_groups(done), swap_groups(own)))
        for n, ref in enumerate((s, om)):
            for k in range(GROUP):
                first, second = tiles_of[0][n][k], tiles_of[1][n][k]
                ref[pl.ds(aligned((p * GROUP + k) * 8), 8), :] = first + pltpu.roll(second, OWN, 1)
        return 0

    lax.fori_loop(0, NP // GROUP, last, 0)

    both = jnp.zeros((2 * NP, NP), F32)
    for x in range(8):
        sx = s[pl.ds(x, NP, stride=8), :]
        share[pl.ds(x * NP, NP), :] = sx
        rows = jnp.concatenate([sx, om[pl.ds(x, NP, stride=8), :]], axis=0)
        both += product(rows, sx, ((1,), (1,)))
    spread = (iota((NP, LANES), 1) % NP == iota((NP, LANES), 0)).astype(F32)
    both = product(both, spread, ((1,), (0,)))
    gram, cross = both[:NP], both[NP:]
    shifted = pltpu.roll(cross, 16, 1)
    lane = iota((8, 128), 1)
    packed = jnp.zeros((8, 128), F32)
    for b in range(4):
        packed = jnp.where(lane // 32 == b, gram[8 * b : 8 * b + 8], packed)
    spare = (lane < 64) & (lane % 32 >= 16)
    for kind in range(4):
        rb, src = kind // 2, (cross if kind % 2 else shifted)
        piece = jnp.where(lane < 32, src[16 * rb : 16 * rb + 8], src[16 * rb + 8 : 16 * rb + 16])
        value = jnp.where(spare, piece, packed)
        for i in range(4):
            msg[pl.ds((4 * i + kind) * 8, 8), :] = value


def sum_kernel(parts, msg):
    n = parts.shape[0] // 8
    s = parts[pl.ds(0, 8), :]
    for g in range(1, n):
        s = s + parts[pl.ds(8 * g, 8), :]
    for d in range(msg.shape[0] // 8):
        msg[pl.ds(8 * d, 8), :] = s


def basis_kernel(parts, share, msg, *, scale):
    n = parts.shape[0] // 8
    s = parts[pl.ds(0, 8), :]
    for g in range(1, n):
        s = s + parts[pl.ds(8 * g, 8), :]
    lane8 = iota((8, 128), 1) // 32
    rows = [all_blocks(jnp.where(lane8 == b, s, 0.0)) for b in range(4)]
    gram = jnp.concatenate(rows, axis=0)
    square = jnp.concatenate([gram] * 4, axis=0)
    flipped = square.T[:NP]
    row, lane = iota((NP, 128), 0), iota((NP, 128), 1)
    a = jnp.where((row < 16) & (lane % 32 >= 16), flipped, gram)
    a = jnp.where(lane < NP, a, jnp.where(lane - NP == row, 1.0, 0.0))
    for j in range(0, NP - 2, 2):
        f0 = jnp.broadcast_to(a[:, j : j + 1], a.shape)
        f1 = jnp.broadcast_to(a[:, j + 1 : j + 2], a.shape)
        r0, r1 = a[j : j + 1], a[j + 1 : j + 2]
        p, q, r = f0[j : j + 1], f0[j + 1 : j + 2], f1[j + 1 : j + 2]
        inv = 1.0 / (p * r - q * q)
        s0, s1 = (r * r0 - q * r1) * inv, (p * r1 - q * r0) * inv
        a = a - jnp.where(row > j + 1, f0 * s0 + f1 * s1, 0.0)
    above = pltpu.roll(a, 1, 0)
    left = lane == row - 1
    p = jnp.sum(jnp.where(left, above, 0.0), axis=1, keepdims=True)
    q = jnp.sum(jnp.where(left, a, 0.0), axis=1, keepdims=True)
    a = jnp.where(row % 2 == 1, a - (q / jnp.where(p > 0.0, p, 1.0)) * above, a)
    diag = jnp.sum(jnp.where(lane == row, a, 0.0), axis=1, keepdims=True)
    inverse = jnp.where(lane // 32 == 1, a * (scale / jnp.sqrt(diag)), 0.0)
    inverse = all_blocks(inverse)
    r = iota((NP, NP), 0)
    pick = (iota((NP, NP), 1) == 2 * (r % 16) + r // 16).astype(F32)
    rows = product(pick, inverse, ((1,), (0,)))[:, :NP]
    for x in range(8):
        out = product(rows, share[pl.ds(x * NP, NP), :], ((1,), (0,)))
        for j in range(2):
            msg[pl.ds(8 * j + x, 16, stride=24), :] = out[16 * j : 16 * j + 16]
    for d in range(16):
        msg[pl.ds(24 * d + 16, 8), :] = s


def finish_kernel(got, basis, core, *, factor):
    lane = iota((8, 128), 1)
    for j in range(2):
        for h in range(2):
            sources = [got[pl.ds(24 * (8 * h + d) + 8 * j, 8), :] for d in range(8)]
            for xt in range(2):
                for l in range(LV):
                    acc = jnp.zeros((8, 128), F32)
                    for d in range(8):
                        shift = (OWN * d - WIN * l - MARGIN - OWN * xt) % LANES
                        acc = jnp.where(lane // OWN == d, pltpu.roll(sources[d], shift, 1), acc)
                    basis[
                        pl.ds((j * LV + l) * RX + 8 * xt, 8), pl.ds(h * LANES, LANES)
                    ] = acc
    rows = []
    for rb in range(2):
        for half in range(2):
            first = 16 + 32 * half
            row = jnp.zeros((8, 128), F32)
            for cb in range(2):
                tile = got[pl.ds((3 * (2 * rb + cb) + 2) * 8, 8), :]
                moved = pltpu.roll(tile, (16 * cb - first) % 128, 1)
                row = jnp.where(lane // 16 == cb, moved, row)
            rows.append(row)
    core[...] = jnp.concatenate(rows, axis=0)[:, :NP] * factor


def shape(*dims):
    return jax.ShapeDtypeStruct(dims, F32)


def call(kernel, specs, outs, scratch=(), cost=None, grant=24 << 20):
    many = isinstance(outs, tuple)
    return pl.pallas_call(
        kernel,
        out_shape=outs,
        in_specs=specs,
        out_specs=(VM,) * len(outs) if many else VM,
        scratch_shapes=list(scratch),
        cost_estimate=cost,
        compiler_params=pltpu.CompilerParams(
            vmem_limit_bytes=grant
        ),
    )


def on_device(probes, wind, station_cell, obs_count, obs_weight):
    tiles, groups = lax.axis_size("space"), lax.axis_size("obs")
    raw, patch, up, down = call(
        prepare_kernel,
        [pl.BlockSpec(memory_space=pltpu.HBM)] * 4 + [SM],
        (
            shape(KINDS * LV * RX, NY),
            shape(NP * RX, LANES),
            shape(MSG, LANES),
            shape(MSG, LANES),
        ),
        (
            pltpu.VMEM((NP * LV * RX, NY), F32),
            pltpu.VMEM((4 * LV * RX, NY), F32),
            pltpu.VMEM(station_cell.shape, jnp.int32),
            pltpu.VMEM(obs_weight.shape, F32),
            pltpu.SemaphoreType.DMA((7,)),
        ),
        grant=60 * 1024 * 1024,
    )(
        probes.reshape(NP * LV * RX, NY),
        wind.reshape(4 * LV * RX, NY),
        station_cell,
        obs_weight,
        obs_count,
    )
    low = lax.ppermute(up, "space", [(i, i + 1) for i in range(tiles - 1)])
    high = lax.ppermute(down, "space", [(i + 1, i) for i in range(tiles - 1)])
    own = call(
        own_kernel,
        [VM],
        shape(groups * KINDS * RX, LANES),
        cost=pl.CostEstimate(flops=2000000, bytes_accessed=4000000, transcendentals=0),
    )(raw)
    msg = call(
        message_kernel,
        [VM] * 3,
        shape(groups * TALL, LANES),
        (pltpu.VMEM((KINDS * LV, 2, 8, LANES), F32),),
    )(own, low, high)
    got = lax.all_to_all(msg.reshape(groups, TALL, LANES), "obs", 0, 0, tiled=True)
    field = pltpu.VMEM((NP * ROWS, LANES), F32)
    padded = pltpu.VMEM((NP * ROWS + 2 * PAD, LANES), F32)
    share, msg = call(
        patch_kernel,
        [VM] * 4,
        (shape(8 * NP, LANES), shape(groups * 8, 128)),
        (
            padded,
            field,
            field,
            field,
            pltpu.VMEM((2 * 7 * LV * SLOT, LANES), F32),
            pltpu.VMEM((UNROLL * LV * SLOT, LANES), F32),
            pltpu.VMEM((UNROLL * LV * SLOT, LANES), F32),
            padded,
            padded,
            padded,
            pltpu.VMEM((NP * 8, LANES), F32),
            pltpu.VMEM((NP * 8, LANES), F32),
        ),
    )(got.reshape(groups * TALL, LANES), patch, low, high)
    got = lax.all_to_all(msg.reshape(groups, 8, 128), "obs", 0, 0, tiled=True)
    msg = call(sum_kernel, [VM], shape(tiles * 8, 128))(got.reshape(groups * 8, 128))
    got = lax.all_to_all(msg.reshape(tiles, 8, 128), "space", 0, 0, tiled=True)
    scale = math.sqrt(LV * RX * tiles * NY)
    msg = call(
        lambda *refs: basis_kernel(*refs, scale=scale), [VM] * 2, shape(groups * 24, LANES)
    )(got.reshape(tiles * 8, 128), share)
    got = lax.all_to_all(msg.reshape(groups, 24, LANES), "obs", 0, 0, tiled=True)
    factor = 1.0 / (groups * tiles * station_cell.shape[1])
    basis, core = call(
        lambda *refs: finish_kernel(*refs, factor=factor),
        [VM],
        (shape(2 * LV * RX, NY), shape(NP, NP)),
    )(got.reshape(groups * 24, LANES))
    return basis.reshape(2, LV, RX, NY), core


def solution(mesh):
    in_specs = (
        P(None, None, "space", None),
        P("obs", None, None, None, "space", None),
        P("obs", "space"),
        P("obs", "space"),
        P("obs", "space"),
    )
    out_specs = (P("obs", None, "space", None), P())
    return jax.shard_map(
        on_device, mesh=mesh, in_specs=in_specs, out_specs=out_specs, check_vma=False
    )
```

```python
import math

import jax
import jax.numpy as jnp
from jax import lax
from jax.experimental import pallas as pl
from jax.experimental.pallas import tpu as pltpu
from jax.sharding import Mesh
from jax.sharding import PartitionSpec as P

F32 = jnp.float32
SPACE = ("z", "core")
HIGH = lax.Precision.HIGHEST
VM = pl.BlockSpec(memory_space=pltpu.VMEM)
SM = pl.BlockSpec(memory_space=pltpu.SMEM)
NT = (((1,), (1,)), ((), ()))

NP, LV, RX, NY = 32, 4, 16, 256
OWN = 16
WIN = 32
MARGIN = 8
HALO = 4
ROWS = RX + 2 * HALO
LANES = 128
GROUP = LANES // WIN
PAD = 8
UNROLL = 8
SLOT = ROWS + 2 * PAD
KINDS = 5
FIRST = (1, 1, 2, 2, 2)
COUNT = tuple(ROWS - 2 * f for f in FIRST)
START = tuple(sum(COUNT[:k]) for k in range(KINDS))
TALL = sum(COUNT)
CHUNK = NP * LV * RX // 4
SIDE = KINDS * LV * HALO
MSG = 2 * SIDE + NP * HALO


def iota(shape, dim):
    return lax.broadcasted_iota(jnp.int32, shape, dim)


def aligned(row):
    return pl.multiple_of(row, 8)


def live_weights(weight_ref, count_ref):
    w = weight_ref[...]
    return jnp.where(iota(w.shape, 1) < count_ref[0, 0], w, 0.0)


def weight_map(cell_row, live):
    cell = cell_row.astype(jnp.int32)
    row, col = cell // NY, cell % NY
    nslot = cell.shape[1]
    on_col = (iota((NY, nslot), 0) == col).astype(jnp.bfloat16)
    on_row = iota((LV * RX, nslot), 0) == row
    total = jnp.zeros((LV * RX, NY), F32)
    rest = live
    for _ in range(3):
        part = rest.astype(jnp.bfloat16).astype(F32)
        rest = rest - part
        lhs = jnp.where(on_row, part, 0.0).astype(jnp.bfloat16)
        total += lax.dot_general(lhs, on_col, NT, preferred_element_type=F32)
    return total


def window(tiles, first):
    shape = tiles[0][0].shape
    lane = iota(shape, 1)
    col = first + lane % WIN
    acc = None
    for k, (lo, hi) in enumerate(tiles):
        if isinstance(first, int) and first + WIN <= LANES:
            both = lo
        elif isinstance(first, int) and first >= LANES:
            both = hi
        else:
            both = jnp.where((lane >= first) & (lane < first + WIN), lo, hi)
        shift = k * WIN - first + 2 * LANES
        shift = shift % LANES if isinstance(first, int) else lax.rem(shift, LANES)
        both = pltpu.roll(both, shift, 1)
        acc = both if acc is None else jnp.where(lane // WIN == k, both, acc)
    return jnp.where((col >= 0) & (col < NY), acc, 0.0)


def prepare_kernel(
    probes_far, wind_far, cells_far, weight_far, count, raw, patch, up, down,
    probes, wind, cells, weight, sems,
):
    copies = [
        pltpu.make_async_copy(far, near, sems.at[i])
        for i, (far, near) in enumerate(
            (
                (cells_far, cells),
                (weight_far, weight),
                (wind_far, wind),
                *(
                    (probes_far.at[pl.ds(c * CHUNK, CHUNK), :], probes.at[pl.ds(c * CHUNK, CHUNK), :])
                    for c in range(4)
                ),
            )
        )
    ]
    for copy in copies:
        copy.start()
    first = lax.axis_index("obs") * OWN - MARGIN
    copies[0].wait()
    copies[1].wait()
    copies[2].wait()
    for i in range(4 * LV):
        raw[pl.ds(i * RX, RX), :] = 0.5 * wind[pl.ds(i * RX, RX), :]
    raw[pl.ds(4 * LV * RX, LV * RX), :] = weight_map(
        cells[...].astype(F32), live_weights(weight, count)
    )

    def one(p, _):
        for l in range(LV):
            for xt in range(2):
                tiles = [
                    [
                        probes[
                            pl.ds(aligned(((p * GROUP + k) * LV + l) * RX + 8 * xt), 8),
                            pl.ds(h * LANES, LANES),
                        ]
                        for h in range(2)
                    ]
                    for k in range(GROUP)
                ]
                patch[pl.ds(aligned((p * LV + l) * RX + 8 * xt), 8), :] = window(tiles, first)
        return 0

    for c in range(4):
        copies[3 + c].wait()
        lax.fori_loop(2 * c, 2 * c + 2, one, 0)
    for out, start in ((up, RX - HALO), (down, 0)):
        for h in range(2):
            for i in range(KINDS * LV):
                out[pl.ds(h * SIDE + i * HALO, HALO), :] = raw[
                    pl.ds(i * RX + start, HALO), pl.ds(h * LANES, LANES)
                ]
        for p in range(NP):
            out[pl.ds(2 * SIDE + p * HALO, HALO), :] = patch[pl.ds(p * RX + start, HALO), :]


def own_kernel(raw, own):
    for kind in range(KINDS):
        for xt in range(2):
            tiles = [
                [
                    raw[pl.ds((kind * LV + l) * RX + 8 * xt, 8), pl.ds(h * LANES, LANES)]
                    for h in range(2)
                ]
                for l in range(LV)
            ]
            for d in range(NY // OWN):
                own[pl.ds((d * KINDS + kind) * RX + 8 * xt, 8), :] = window(
                    tiles, d * OWN - MARGIN
                )


def message_kernel(own, low, high, msg, edge):
    for h in range(2):
        for i in range(KINDS * LV):
            src = pl.ds(h * SIDE + i * HALO, HALO)
            edge[i, h, pl.ds(0, HALO), :] = low[src, :]
            edge[i, h, pl.ds(HALO, HALO), :] = high[src, :]
    for kind in range(KINDS):
        tiles = [[edge[kind * LV + l, h] for h in range(2)] for l in range(LV)]
        for d in range(NY // OWN):
            value = window(tiles, d * OWN - MARGIN)
            base, n = d * TALL + START[kind], HALO - FIRST[kind]
            msg[pl.ds(base, n), :] = value[HALO - n : HALO]
            msg[pl.ds(base + n, RX), :] = own[pl.ds((d * KINDS + kind) * RX, RX), :]
            msg[pl.ds(base + n + RX, n), :] = value[HALO : HALO + n]


def all_blocks(t):
    return t + pltpu.roll(t, 32, 1) + pltpu.roll(t, 64, 1) + pltpu.roll(t, 96, 1)


def product(a, b, dims):
    return lax.dot_general(a, b, (dims, ((), ())), precision=HIGH, preferred_element_type=F32)


def level_sum(c, l):
    if l == 0:
        return c[1]
    if l == LV - 1:
        return c[l - 1]
    return c[l - 1] + c[l + 1]


def swap_groups(v):
    lane = iota(v[0].shape, 1)
    low, even = lane < 64, lane // 32 % 2 == 0

    def half(w):
        return pltpu.roll(w, 64, 1)

    x = [
        jnp.where(low, v[0], half(v[2])),
        jnp.where(low, v[1], half(v[3])),
        jnp.where(low, half(v[0]), v[2]),
        jnp.where(low, half(v[1]), v[3]),
    ]
    out = []
    for a in (0, 2):
        out.append(jnp.where(even, x[a], pltpu.roll(x[a + 1], 32, 1)))
        out.append(jnp.where(even, pltpu.roll(x[a], 96, 1), x[a + 1]))
    return out


def patch_kernel(
    got, patch, low, high, share, msg, u, au, dx, dy, cf, t1, t2, va, pa, qa, s, om
):
    t, o = lax.axis_index(SPACE), lax.axis_index("obs")
    tiles = lax.axis_size(SPACE)
    lane = iota((8, LANES), 1)
    col = o * OWN - MARGIN + lane % WIN
    inside = []
    for i in range(3):
        row = t * RX - HALO + 8 * i + iota((8, LANES), 0)
        inside.append((row >= 0) & (row < tiles * RX) & (col >= 0) & (col < NY))

    def right(c):
        return pltpu.roll(c, LANES - 1, 1)

    def left(c):
        return pltpu.roll(c, 1, 1)

    def levels(c, l):
        return 0.2 * c[l] + 0.1 * level_sum(c, l)

    def tenfold(c, l):
        return (c[l] + c[l]) + level_sum(c, l)

    edge = jnp.zeros((PAD, LANES), F32)
    for ref in (u, va, pa, qa):
        ref[pl.ds(0, PAD), :] = edge
        ref[pl.ds(PAD + NP * ROWS, PAD), :] = edge
    cf[...] = jnp.zeros(cf.shape, F32)
    for ref, n in ((t1, UNROLL * LV), (t2, UNROLL * LV)):
        for j in range(n):
            ref[pl.ds(j * SLOT, PAD), :] = edge
            ref[pl.ds(j * SLOT + PAD + ROWS, PAD), :] = edge
    for f in range(NP):
        base = PAD + f * ROWS
        u[pl.ds(base, HALO), :] = low[pl.ds(2 * SIDE + f * HALO, HALO), :]
        u[pl.ds(base + HALO, RX), :] = patch[pl.ds(f * RX, RX), :]
        u[pl.ds(base + HALO + RX, HALO), :] = high[pl.ds(2 * SIDE + f * HALO, HALO), :]

    def shared(p, _):
        for i in range(3):
            at = [aligned((p * LV + l) * ROWS + 8 * i) for l in range(LV)]
            c = [u[pl.ds(at[l] + PAD, 8), :] for l in range(LV)]
            for l in range(LV):
                xp, xm = u[pl.ds(at[l] + PAD + 1, 8), :], u[pl.ds(at[l] + PAD - 1, 8), :]
                yp, ym = right(c[l]), left(c[l])
                mean = 0.01 * tenfold(c, l) + 0.015 * ((xp + xm) + (yp + ym))
                here = pl.ds(at[l], 8)
                au[here, :] = jnp.where(inside[i], mean, 0.0)
                dx[here, :] = jnp.where(inside[i], 0.1 * (xp - xm), 0.0)
                dy[here, :] = jnp.where(inside[i], 0.1 * (yp - ym), 0.0)
                for ref in (va, pa, qa):
                    ref[pl.ds(at[l] + PAD, 8), :] = edge
        return 0

    lax.fori_loop(0, NP // GROUP, shared, 0, unroll=2)

    def place(turn, j, l):
        return ((turn * 7 + j) * LV + l) * SLOT

    def expand(g, turn):
        base = g * TALL
        for kind in range(KINDS):
            for off in (0, 8, COUNT[kind] - 8):
                tile = got[pl.ds(base + START[kind] + off, 8), :]
                row = PAD + FIRST[kind] + off
                for l in range(LV):
                    m = jnp.take_along_axis(tile, l * WIN + lane % WIN, axis=1)
                    if kind in (2, 3):
                        m = 10.0 * m
                        pair = ((2 * kind - 4, 1.5 - m), (2 * kind - 3, 1.5 + m))
                    else:
                        pair = (({0: 4, 1: 5, 4: 6}[kind], 0.1 * m if kind == 4 else m),)
                    for j, value in pair:
                        cf[pl.ds(place(turn, j, l) + row, 8), :] = value

    def steps(turn):
        def coef(j, l, i, off=0):
            return cf[pl.ds(place(turn, j, l) + PAD + 8 * i + off, 8), :]

        def some(step, _):
            slots = range(UNROLL)

            def at(q, l, i):
                return aligned(((step * UNROLL + q) * LV + l) * ROWS + 8 * i)

            def slot(q, l, i, off=0):
                return pl.ds((q * LV + l) * SLOT + PAD + 8 * i + off, 8)

            for i in range(3):
                for l in range(LV):
                    a, b = coef(4, l, i), coef(5, l, i)
                    for q in slots:
                        here = pl.ds(at(q, l, i), 8)
                        t1[slot(q, l, i), :] = au[here, :] - a * dx[here, :] - b * dy[here, :]
            for i in range(3):
                c = [[t1[slot(q, l, i), :] for l in range(LV)] for q in slots]
                for l in range(LV):
                    cxp, cxm, cyp, cym = (coef(j, l, i) for j in range(4))
                    w = coef(6, l, i)
                    for q in slots:
                        r = tenfold(c[q], l)
                        r += cxp * t1[slot(q, l, i, 1), :] + cxm * t1[slot(q, l, i, -1), :]
                        r += cyp * right(c[q][l]) + cym * left(c[q][l])
                        t2[slot(q, l, i), :] = w * r
            for i in range(3):
                c = [[t2[slot(q, l, i), :] for l in range(LV)] for q in slots]
                for l in range(LV):
                    cxp, cxm = coef(0, l, i, -1), coef(1, l, i, 1)
                    cyp, cym = coef(2, l, i), coef(3, l, i)
                    a, b = coef(4, l, i), coef(5, l, i)
                    for q in slots:
                        r = tenfold(c[q], l)
                        r += cxm * t2[slot(q, l, i, 1), :] + cxp * t2[slot(q, l, i, -1), :]
                        r += right(cym * c[q][l]) + left(cyp * c[q][l])
                        here = pl.ds(at(q, l, i) + PAD, 8)
                        va[here, :] += r
                        pa[here, :] += a * r
                        qa[here, :] += b * r
            return 0

        if UNROLL == NP // GROUP:
            some(0, 0)
        else:
            lax.fori_loop(0, NP // GROUP // UNROLL, some, 0)

    windows = got.shape[0] // TALL
    expand(0, 0)

    def two_windows(h, _):
        expand(2 * h + 1, 1)
        steps(0)
        expand(jnp.minimum(2 * h + 2, windows - 1), 0)
        steps(1)
        return 0

    lax.fori_loop(0, windows // 2, two_windows, 0)

    def mask(f, _):
        for i in range(3):
            at = pl.ds(aligned(PAD + f * ROWS + 8 * i), 8)
            for ref in (va, pa, qa):
                ref[at, :] = jnp.where(inside[i], ref[at, :], 0.0)
        return 0

    lax.fori_loop(0, NP, mask, 0, unroll=4)
    core_lane = (lane % WIN >= MARGIN) & (lane % WIN < MARGIN + OWN)

    def last(p, _):
        tiles_of = []
        for i in range(2):
            at = [aligned(PAD + (p * LV + l) * ROWS + 8 * i) + HALO for l in range(LV)]
            c = [va[pl.ds(at[l], 8), :] for l in range(LV)]
            done = []
            for l in range(LV):
                q = qa[pl.ds(at[l], 8), :]
                r = levels(c, l)
                xs = va[pl.ds(at[l] + 1, 8), :] + va[pl.ds(at[l] - 1, 8), :]
                r += 0.15 * (xs + (right(c[l]) + left(c[l])))
                r += (pa[pl.ds(at[l] + 1, 8), :] - pa[pl.ds(at[l] - 1, 8), :]) + (
                    right(q) - left(q)
                )
                done.append(jnp.where(core_lane, r, 0.0))
            own = [jnp.where(core_lane, u[pl.ds(at[l], 8), :], 0.0) for l in range(LV)]
            tiles_of.append((swap_groups(done), swap_groups(own)))
        for n, ref in enumerate((s, om)):
            for k in range(GROUP):
                first, second = tiles_of[0][n][k], tiles_of[1][n][k]
                ref[pl.ds(aligned((p * GROUP + k) * 8), 8), :] = first + pltpu.roll(second, OWN, 1)
        return 0

    lax.fori_loop(0, NP // GROUP, last, 0, unroll=2)

    both = jnp.zeros((2 * NP, NP), F32)
    for x in range(8):
        sx = s[pl.ds(x, NP, stride=8), :]
        share[pl.ds(x * NP, NP), :] = sx
        rows = jnp.concatenate([sx, om[pl.ds(x, NP, stride=8), :]], axis=0)
        both += product(rows, sx, ((1,), (1,)))
    spread = (iota((NP, LANES), 1) % NP == iota((NP, LANES), 0)).astype(F32)
    both = product(both, spread, ((1,), (0,)))
    gram, cross = both[:NP], both[NP:]
    shifted = pltpu.roll(cross, 16, 1)
    lane = iota((8, 128), 1)
    packed = jnp.zeros((8, 128), F32)
    for b in range(4):
        packed = jnp.where(lane // 32 == b, gram[8 * b : 8 * b + 8], packed)
    spare = (lane < 64) & (lane % 32 >= 16)
    for kind in range(4):
        rb, src = kind // 2, (cross if kind % 2 else shifted)
        piece = jnp.where(lane < 32, src[16 * rb : 16 * rb + 8], src[16 * rb + 8 : 16 * rb + 16])
        value = jnp.where(spare, piece, packed)
        for i in range(4):
            for core in range(2):
                msg[pl.ds((2 * (4 * i + kind) + core) * 8, 8), :] = value


def sum_kernel(parts, msg):
    n = parts.shape[0] // 8
    s = parts[pl.ds(0, 8), :]
    for g in range(1, n):
        s = s + parts[pl.ds(8 * g, 8), :]
    for d in range(msg.shape[0] // 8):
        msg[pl.ds(8 * d, 8), :] = s


def basis_kernel(parts, share, msg, *, scale):
    n = parts.shape[0] // 8
    s = parts[pl.ds(0, 8), :]
    for g in range(1, n):
        s = s + parts[pl.ds(8 * g, 8), :]
    lane8 = iota((8, 128), 1) // 32
    rows = [all_blocks(jnp.where(lane8 == b, s, 0.0)) for b in range(4)]
    gram = jnp.concatenate(rows, axis=0)
    square = jnp.concatenate([gram] * 4, axis=0)
    flipped = square.T[:NP]
    row, lane = iota((NP, 128), 0), iota((NP, 128), 1)
    a = jnp.where((row < 16) & (lane % 32 >= 16), flipped, gram)
    a = jnp.where(lane < NP, a, jnp.where(lane - NP == row, 1.0, 0.0))
    for j in range(0, NP - 2, 2):
        f0 = jnp.broadcast_to(a[:, j : j + 1], a.shape)
        f1 = jnp.broadcast_to(a[:, j + 1 : j + 2], a.shape)
        r0, r1 = a[j : j + 1], a[j + 1 : j + 2]
        p, q, r = f0[j : j + 1], f0[j + 1 : j + 2], f1[j + 1 : j + 2]
        inv = 1.0 / (p * r - q * q)
        s0, s1 = (r * r0 - q * r1) * inv, (p * r1 - q * r0) * inv
        a = a - jnp.where(row > j + 1, f0 * s0 + f1 * s1, 0.0)
    above = pltpu.roll(a, 1, 0)
    left = lane == row - 1
    p = jnp.sum(jnp.where(left, above, 0.0), axis=1, keepdims=True)
    q = jnp.sum(jnp.where(left, a, 0.0), axis=1, keepdims=True)
    a = jnp.where(row % 2 == 1, a - (q / jnp.where(p > 0.0, p, 1.0)) * above, a)
    diag = jnp.sum(jnp.where(lane == row, a, 0.0), axis=1, keepdims=True)
    inverse = jnp.where(lane // 32 == 1, a * (scale / jnp.sqrt(diag)), 0.0)
    inverse = all_blocks(inverse)
    r = iota((NP, NP), 0)
    pick = (iota((NP, NP), 1) == 2 * (r % 16) + r // 16).astype(F32)
    rows = product(pick, inverse, ((1,), (0,)))[:, :NP]
    for x in range(8):
        out = product(rows, share[pl.ds(x * NP, NP), :], ((1,), (0,)))
        for j in range(2):
            msg[pl.ds(8 * j + x, 16, stride=24), :] = out[16 * j : 16 * j + 16]
    for d in range(16):
        msg[pl.ds(24 * d + 16, 8), :] = s


def finish_kernel(got, basis, core, *, factor):
    lane = iota((8, 128), 1)
    for j in range(2):
        for h in range(2):
            sources = [got[pl.ds(24 * (8 * h + d) + 8 * j, 8), :] for d in range(8)]
            for xt in range(2):
                for l in range(LV):
                    acc = jnp.zeros((8, 128), F32)
                    for d in range(8):
                        shift = (OWN * d - WIN * l - MARGIN - OWN * xt) % LANES
                        acc = jnp.where(lane // OWN == d, pltpu.roll(sources[d], shift, 1), acc)
                    basis[
                        pl.ds((j * LV + l) * RX + 8 * xt, 8), pl.ds(h * LANES, LANES)
                    ] = acc
    rows = []
    for rb in range(2):
        for half in range(2):
            first = 16 + 32 * half
            row = jnp.zeros((8, 128), F32)
            for cb in range(2):
                tile = got[pl.ds((3 * (2 * rb + cb) + 2) * 8, 8), :]
                moved = pltpu.roll(tile, (16 * cb - first) % 128, 1)
                row = jnp.where(lane // 16 == cb, moved, row)
            rows.append(row)
    core[...] = jnp.concatenate(rows, axis=0)[:, :NP] * factor


def shape(*dims):
    return jax.ShapeDtypeStruct(dims, F32)


def call(kernel, specs, outs, scratch=(), cost=None, grant=24 << 20):
    many = isinstance(outs, tuple)
    return pl.pallas_call(
        kernel,
        out_shape=outs,
        in_specs=specs,
        out_specs=(VM,) * len(outs) if many else VM,
        scratch_shapes=list(scratch),
        cost_estimate=cost,
        compiler_params=pltpu.CompilerParams(
            vmem_limit_bytes=grant
        ),
    )


def on_device(probes, wind, station_cell, obs_count, obs_weight):
    tiles, groups = lax.axis_size(SPACE), lax.axis_size("obs")
    layers, plane = lax.axis_size("z"), 2 * groups
    raw, patch, up, down = call(
        prepare_kernel,
        [pl.BlockSpec(memory_space=pltpu.HBM)] * 4 + [SM],
        (
            shape(KINDS * LV * RX, NY),
            shape(NP * RX, LANES),
            shape(MSG, LANES),
            shape(MSG, LANES),
        ),
        (
            pltpu.VMEM((NP * LV * RX, NY), F32),
            pltpu.VMEM((4 * LV * RX, NY), F32),
            pltpu.VMEM(station_cell.shape, jnp.int32),
            pltpu.VMEM(obs_weight.shape, F32),
            pltpu.SemaphoreType.DMA((7,)),
        ),
        grant=60 * 1024 * 1024,
    )(
        probes.reshape(NP * LV * RX, NY),
        wind.reshape(4 * LV * RX, NY),
        station_cell,
        obs_weight,
        obs_count,
    )
    low = lax.ppermute(up, SPACE, [(i, i + 1) for i in range(tiles - 1)])
    high = lax.ppermute(down, SPACE, [(i + 1, i) for i in range(tiles - 1)])
    own = call(
        own_kernel,
        [VM],
        shape(groups * KINDS * RX, LANES),
        cost=pl.CostEstimate(flops=2000000, bytes_accessed=4000000, transcendentals=0),
    )(raw)
    msg = call(
        message_kernel,
        [VM] * 3,
        shape(groups * TALL, LANES),
        (pltpu.VMEM((KINDS * LV, 2, 8, LANES), F32),),
    )(own, low, high)
    got = lax.all_to_all(msg.reshape(groups, TALL, LANES), "obs", 0, 0, tiled=True)
    field = pltpu.VMEM((NP * ROWS, LANES), F32)
    padded = pltpu.VMEM((NP * ROWS + 2 * PAD, LANES), F32)
    share, msg = call(
        patch_kernel,
        [VM] * 4,
        (shape(8 * NP, LANES), shape(plane * 8, 128)),
        (
            padded,
            field,
            field,
            field,
            pltpu.VMEM((2 * 7 * LV * SLOT, LANES), F32),
            pltpu.VMEM((UNROLL * LV * SLOT, LANES), F32),
            pltpu.VMEM((UNROLL * LV * SLOT, LANES), F32),
            padded,
            padded,
            padded,
            pltpu.VMEM((NP * 8, LANES), F32),
            pltpu.VMEM((NP * 8, LANES), F32),
        ),
    )(got.reshape(groups * TALL, LANES), patch, low, high)
    got = lax.all_to_all(msg.reshape(plane, 8, 128), ("obs", "core"), 0, 0, tiled=True)
    msg = call(sum_kernel, [VM], shape(layers * 8, 128))(got.reshape(plane * 8, 128))
    got = lax.all_to_all(msg.reshape(layers, 8, 128), "z", 0, 0, tiled=True)
    scale = math.sqrt(LV * RX * tiles * NY)
    msg = call(
        lambda *refs: basis_kernel(*refs, scale=scale), [VM] * 2, shape(groups * 24, LANES)
    )(got.reshape(layers * 8, 128), share)
    got = lax.all_to_all(msg.reshape(groups, 24, LANES), "obs", 0, 0, tiled=True)
    factor = 1.0 / (groups * tiles * station_cell.shape[1])
    basis, core = call(
        lambda *refs: finish_kernel(*refs, factor=factor),
        [VM],
        (shape(2 * LV * RX, NY), shape(NP, NP)),
    )(got.reshape(groups * 24, LANES))
    return basis.reshape(2, LV, RX, NY), core


def solution(mesh):
    groups, tiles = mesh.shape["obs"], mesh.shape["space"]
    split = Mesh(mesh.devices.reshape(groups, tiles // 2, 2), ("obs", *SPACE))
    in_specs = (
        P(None, None, SPACE, None),
        P("obs", None, None, None, SPACE, None),
        P("obs", SPACE),
        P("obs", SPACE),
        P("obs", SPACE),
    )
    out_specs = (P("obs", None, SPACE, None), P())
    return jax.shard_map(
        on_device, mesh=split, in_specs=in_specs, out_specs=out_specs, check_vma=False
    )
```

```python
import math

import jax
import jax.numpy as jnp
from jax import lax
from jax.experimental import pallas as pl
from jax.experimental.pallas import tpu as pltpu
from jax.sharding import Mesh
from jax.sharding import PartitionSpec as P

F32 = jnp.float32
SPACE = ("z", "core")
HIGH = lax.Precision.HIGHEST
VM = pl.BlockSpec(memory_space=pltpu.VMEM)
SM = pl.BlockSpec(memory_space=pltpu.SMEM)
NT = (((1,), (1,)), ((), ()))

NP, LV, RX, NY = 32, 4, 16, 256
OWN = 16
WIN = 32
MARGIN = 8
HALO = 4
ROWS = RX + 2 * HALO
LANES = 128
GROUP = LANES // WIN
PAD = 8
UNROLL = 8
SLOT = ROWS + 2 * PAD
KINDS = 5
FIRST = (1, 1, 2, 2, 2)
COUNT = tuple(ROWS - 2 * f for f in FIRST)
START = tuple(sum(COUNT[:k]) for k in range(KINDS))
TALL = sum(COUNT)
CHUNK = NP * LV * RX // 4
SIDE = KINDS * LV * HALO
MSG = 2 * SIDE + NP * HALO


def iota(shape, dim):
    return lax.broadcasted_iota(jnp.int32, shape, dim)


def aligned(row):
    return pl.multiple_of(row, 8)


def live_weights(weight_ref, count_ref):
    w = weight_ref[...]
    return jnp.where(iota(w.shape, 1) < count_ref[0, 0], w, 0.0)


def weight_map(cell_row, live):
    cell = cell_row.astype(jnp.int32)
    row, col = cell // NY, cell % NY
    nslot = cell.shape[1]
    on_col = (iota((NY, nslot), 0) == col).astype(jnp.bfloat16)
    on_row = iota((LV * RX, nslot), 0) == row
    total = jnp.zeros((LV * RX, NY), F32)
    rest = live
    for _ in range(3):
        part = rest.astype(jnp.bfloat16).astype(F32)
        rest = rest - part
        lhs = jnp.where(on_row, part, 0.0).astype(jnp.bfloat16)
        total += lax.dot_general(lhs, on_col, NT, preferred_element_type=F32)
    return total


def window(tiles, first):
    shape = tiles[0][0].shape
    lane = iota(shape, 1)
    col = first + lane % WIN
    acc = None
    for k, (lo, hi) in enumerate(tiles):
        if isinstance(first, int) and first + WIN <= LANES:
            both = lo
        elif isinstance(first, int) and first >= LANES:
            both = hi
        else:
            both = jnp.where((lane >= first) & (lane < first + WIN), lo, hi)
        shift = k * WIN - first + 2 * LANES
        shift = shift % LANES if isinstance(first, int) else lax.rem(shift, LANES)
        both = pltpu.roll(both, shift, 1)
        acc = both if acc is None else jnp.where(lane // WIN == k, both, acc)
    return jnp.where((col >= 0) & (col < NY), acc, 0.0)


def prepare_kernel(
    probes_far, wind_far, cells_far, weight_far, count, raw, patch, inner, outer,
    probes, wind, cells, weight, sems,
):
    copies = [
        pltpu.make_async_copy(far, near, sems.at[i])
        for i, (far, near) in enumerate(
            (
                (cells_far, cells),
                (weight_far, weight),
                (wind_far, wind),
                *(
                    (probes_far.at[pl.ds(c * CHUNK, CHUNK), :], probes.at[pl.ds(c * CHUNK, CHUNK), :])
                    for c in range(4)
                ),
            )
        )
    ]
    for copy in copies:
        copy.start()
    first = lax.axis_index("obs") * OWN - MARGIN
    copies[0].wait()
    copies[1].wait()
    copies[2].wait()
    for i in range(4 * LV):
        raw[pl.ds(i * RX, RX), :] = 0.5 * wind[pl.ds(i * RX, RX), :]
    raw[pl.ds(4 * LV * RX, LV * RX), :] = weight_map(
        cells[...].astype(F32), live_weights(weight, count)
    )

    def one(p, _):
        for l in range(LV):
            for xt in range(2):
                tiles = [
                    [
                        probes[
                            pl.ds(aligned(((p * GROUP + k) * LV + l) * RX + 8 * xt), 8),
                            pl.ds(h * LANES, LANES),
                        ]
                        for h in range(2)
                    ]
                    for k in range(GROUP)
                ]
                patch[pl.ds(aligned((p * LV + l) * RX + 8 * xt), 8), :] = window(tiles, first)
        return 0

    for c in range(4):
        copies[3 + c].wait()
        lax.fori_loop(2 * c, 2 * c + 2, one, 0)
    low_core = lax.axis_index("core") == 0

    def either(ref, row, cols, for_inner):
        top, bottom = ref[pl.ds(row + RX - HALO, HALO), cols], ref[pl.ds(row, HALO), cols]
        return jnp.where(low_core == for_inner, top, bottom)

    for out, for_inner in ((inner, True), (outer, False)):
        for h in range(2):
            for i in range(KINDS * LV):
                out[pl.ds(h * SIDE + i * HALO, HALO), :] = either(
                    raw, i * RX, pl.ds(h * LANES, LANES), for_inner
                )
        for p in range(NP):
            out[pl.ds(2 * SIDE + p * HALO, HALO), :] = either(
                patch, p * RX, slice(None), for_inner
            )


def own_kernel(raw, own):
    for kind in range(KINDS):
        for xt in range(2):
            tiles = [
                [
                    raw[pl.ds((kind * LV + l) * RX + 8 * xt, 8), pl.ds(h * LANES, LANES)]
                    for h in range(2)
                ]
                for l in range(LV)
            ]
            for d in range(NY // OWN):
                own[pl.ds((d * KINDS + kind) * RX + 8 * xt, 8), :] = window(
                    tiles, d * OWN - MARGIN
                )


def message_kernel(own, inner, outer, msg, edge):
    low_core = lax.axis_index("core") == 0
    for h in range(2):
        for i in range(KINDS * LV):
            src = pl.ds(h * SIDE + i * HALO, HALO)
            near, far = inner[src, :], outer[src, :]
            edge[i, h, pl.ds(0, HALO), :] = jnp.where(low_core, far, near)
            edge[i, h, pl.ds(HALO, HALO), :] = jnp.where(low_core, near, far)
    for kind in range(KINDS):
        tiles = [[edge[kind * LV + l, h] for h in range(2)] for l in range(LV)]
        for d in range(NY // OWN):
            value = window(tiles, d * OWN - MARGIN)
            base, n = d * TALL + START[kind], HALO - FIRST[kind]
            msg[pl.ds(base, n), :] = value[HALO - n : HALO]
            msg[pl.ds(base + n, RX), :] = own[pl.ds((d * KINDS + kind) * RX, RX), :]
            msg[pl.ds(base + n + RX, n), :] = value[HALO : HALO + n]


def all_blocks(t):
    return t + pltpu.roll(t, 32, 1) + pltpu.roll(t, 64, 1) + pltpu.roll(t, 96, 1)


def product(a, b, dims):
    return lax.dot_general(a, b, (dims, ((), ())), precision=HIGH, preferred_element_type=F32)


def level_sum(c, l):
    if l == 0:
        return c[1]
    if l == LV - 1:
        return c[l - 1]
    return c[l - 1] + c[l + 1]


def swap_groups(v):
    lane = iota(v[0].shape, 1)
    low, even = lane < 64, lane // 32 % 2 == 0

    def half(w):
        return pltpu.roll(w, 64, 1)

    x = [
        jnp.where(low, v[0], half(v[2])),
        jnp.where(low, v[1], half(v[3])),
        jnp.where(low, half(v[0]), v[2]),
        jnp.where(low, half(v[1]), v[3]),
    ]
    out = []
    for a in (0, 2):
        out.append(jnp.where(even, x[a], pltpu.roll(x[a + 1], 32, 1)))
        out.append(jnp.where(even, pltpu.roll(x[a], 96, 1), x[a + 1]))
    return out


def patch_kernel(
    got, patch, inner, outer, share, msg, u, au, dx, dy, cf, t1, t2, va, pa, qa, s, om
):
    t, o = lax.axis_index(SPACE), lax.axis_index("obs")
    tiles = lax.axis_size(SPACE)
    low_core = lax.axis_index("core") == 0
    lane = iota((8, LANES), 1)
    col = o * OWN - MARGIN + lane % WIN
    inside = []
    for i in range(3):
        row = t * RX - HALO + 8 * i + iota((8, LANES), 0)
        inside.append((row >= 0) & (row < tiles * RX) & (col >= 0) & (col < NY))

    def right(c):
        return pltpu.roll(c, LANES - 1, 1)

    def left(c):
        return pltpu.roll(c, 1, 1)

    def levels(c, l):
        return 0.2 * c[l] + 0.1 * level_sum(c, l)

    def tenfold(c, l):
        return (c[l] + c[l]) + level_sum(c, l)

    edge = jnp.zeros((PAD, LANES), F32)
    for ref in (u, va, pa, qa):
        ref[pl.ds(0, PAD), :] = edge
        ref[pl.ds(PAD + NP * ROWS, PAD), :] = edge
    cf[...] = jnp.zeros(cf.shape, F32)
    for ref, n in ((t1, UNROLL * LV), (t2, UNROLL * LV)):
        for j in range(n):
            ref[pl.ds(j * SLOT, PAD), :] = edge
            ref[pl.ds(j * SLOT + PAD + ROWS, PAD), :] = edge
    for f in range(NP):
        base = PAD + f * ROWS
        src = pl.ds(2 * SIDE + f * HALO, HALO)
        near, far = inner[src, :], outer[src, :]
        u[pl.ds(base, HALO), :] = jnp.where(low_core, far, near)
        u[pl.ds(base + HALO, RX), :] = patch[pl.ds(f * RX, RX), :]
        u[pl.ds(base + HALO + RX, HALO), :] = jnp.where(low_core, near, far)

    def shared(p, _):
        for i in range(3):
            at = [aligned((p * LV + l) * ROWS + 8 * i) for l in range(LV)]
            c = [u[pl.ds(at[l] + PAD, 8), :] for l in range(LV)]
            for l in range(LV):
                xp, xm = u[pl.ds(at[l] + PAD + 1, 8), :], u[pl.ds(at[l] + PAD - 1, 8), :]
                yp, ym = right(c[l]), left(c[l])
                mean = 0.01 * tenfold(c, l) + 0.015 * ((xp + xm) + (yp + ym))
                here = pl.ds(at[l], 8)
                au[here, :] = jnp.where(inside[i], mean, 0.0)
                dx[here, :] = jnp.where(inside[i], 0.1 * (xp - xm), 0.0)
                dy[here, :] = jnp.where(inside[i], 0.1 * (yp - ym), 0.0)
                for ref in (va, pa, qa):
                    ref[pl.ds(at[l] + PAD, 8), :] = edge
        return 0

    lax.fori_loop(0, NP // GROUP, shared, 0, unroll=2)

    def place(turn, j, l):
        return ((turn * 7 + j) * LV + l) * SLOT

    def expand(g, turn):
        base = g * TALL
        for kind in range(KINDS):
            for off in (0, 8, COUNT[kind] - 8):
                tile = got[pl.ds(base + START[kind] + off, 8), :]
                row = PAD + FIRST[kind] + off
                for l in range(LV):
                    m = jnp.take_along_axis(tile, l * WIN + lane % WIN, axis=1)
                    if kind in (2, 3):
                        m = 10.0 * m
                        pair = ((2 * kind - 4, 1.5 - m), (2 * kind - 3, 1.5 + m))
                    else:
                        pair = (({0: 4, 1: 5, 4: 6}[kind], 0.1 * m if kind == 4 else m),)
                    for j, value in pair:
                        cf[pl.ds(place(turn, j, l) + row, 8), :] = value

    def steps(turn):
        def coef(j, l, i, off=0):
            return cf[pl.ds(place(turn, j, l) + PAD + 8 * i + off, 8), :]

        def some(step, _):
            slots = range(UNROLL)

            def at(q, l, i):
                return aligned(((step * UNROLL + q) * LV + l) * ROWS + 8 * i)

            def slot(q, l, i, off=0):
                return pl.ds((q * LV + l) * SLOT + PAD + 8 * i + off, 8)

            for i in range(3):
                for l in range(LV):
                    a, b = coef(4, l, i), coef(5, l, i)
                    for q in slots:
                        here = pl.ds(at(q, l, i), 8)
                        t1[slot(q, l, i), :] = au[here, :] - a * dx[here, :] - b * dy[here, :]
            for i in range(3):
                c = [[t1[slot(q, l, i), :] for l in range(LV)] for q in slots]
                for l in range(LV):
                    cxp, cxm, cyp, cym = (coef(j, l, i) for j in range(4))
                    w = coef(6, l, i)
                    for q in slots:
                        r = tenfold(c[q], l)
                        r += cxp * t1[slot(q, l, i, 1), :] + cxm * t1[slot(q, l, i, -1), :]
                        r += cyp * right(c[q][l]) + cym * left(c[q][l])
                        t2[slot(q, l, i), :] = w * r
            for i in range(3):
                c = [[t2[slot(q, l, i), :] for l in range(LV)] for q in slots]
                for l in range(LV):
                    cxp, cxm = coef(0, l, i, -1), coef(1, l, i, 1)
                    cyp, cym = coef(2, l, i), coef(3, l, i)
                    a, b = coef(4, l, i), coef(5, l, i)
                    for q in slots:
                        r = tenfold(c[q], l)
                        r += cxm * t2[slot(q, l, i, 1), :] + cxp * t2[slot(q, l, i, -1), :]
                        r += right(cym * c[q][l]) + left(cyp * c[q][l])
                        here = pl.ds(at(q, l, i) + PAD, 8)
                        va[here, :] += r
                        pa[here, :] += a * r
                        qa[here, :] += b * r
            return 0

        if UNROLL == NP // GROUP:
            some(0, 0)
        else:
            lax.fori_loop(0, NP // GROUP // UNROLL, some, 0)

    windows = got.shape[0] // TALL
    expand(0, 0)

    def two_windows(h, _):
        expand(2 * h + 1, 1)
        steps(0)
        expand(jnp.minimum(2 * h + 2, windows - 1), 0)
        steps(1)
        return 0

    lax.fori_loop(0, windows // 2, two_windows, 0)

    def mask(f, _):
        for i in range(3):
            at = pl.ds(aligned(PAD + f * ROWS + 8 * i), 8)
            for ref in (va, pa, qa):
                ref[at, :] = jnp.where(inside[i], ref[at, :], 0.0)
        return 0

    lax.fori_loop(0, NP, mask, 0, unroll=4)
    core_lane = (lane % WIN >= MARGIN) & (lane % WIN < MARGIN + OWN)

    def last(p, _):
        tiles_of = []
        for i in range(2):
            at = [aligned(PAD + (p * LV + l) * ROWS + 8 * i) + HALO for l in range(LV)]
            c = [va[pl.ds(at[l], 8), :] for l in range(LV)]
            done = []
            for l in range(LV):
                q = qa[pl.ds(at[l], 8), :]
                r = levels(c, l)
                xs = va[pl.ds(at[l] + 1, 8), :] + va[pl.ds(at[l] - 1, 8), :]
                r += 0.15 * (xs + (right(c[l]) + left(c[l])))
                r += (pa[pl.ds(at[l] + 1, 8), :] - pa[pl.ds(at[l] - 1, 8), :]) + (
                    right(q) - left(q)
                )
                done.append(jnp.where(core_lane, r, 0.0))
            own = [jnp.where(core_lane, u[pl.ds(at[l], 8), :], 0.0) for l in range(LV)]
            tiles_of.append((swap_groups(done), swap_groups(own)))
        for n, ref in enumerate((s, om)):
            for k in range(GROUP):
                first, second = tiles_of[0][n][k], tiles_of[1][n][k]
                ref[pl.ds(aligned((p * GROUP + k) * 8), 8), :] = first + pltpu.roll(second, OWN, 1)
        return 0

    lax.fori_loop(0, NP // GROUP, last, 0, unroll=2)

    both = jnp.zeros((2 * NP, NP), F32)
    for x in range(8):
        sx = s[pl.ds(x, NP, stride=8), :]
        share[pl.ds(x * NP, NP), :] = sx
        rows = jnp.concatenate([sx, om[pl.ds(x, NP, stride=8), :]], axis=0)
        both += product(rows, sx, ((1,), (1,)))
    spread = (iota((NP, LANES), 1) % NP == iota((NP, LANES), 0)).astype(F32)
    both = product(both, spread, ((1,), (0,)))
    gram, cross = both[:NP], both[NP:]
    shifted = pltpu.roll(cross, 16, 1)
    lane = iota((8, 128), 1)
    packed = jnp.zeros((8, 128), F32)
    for b in range(4):
        packed = jnp.where(lane // 32 == b, gram[8 * b : 8 * b + 8], packed)
    spare = (lane < 64) & (lane % 32 >= 16)
    for kind in range(4):
        rb, src = kind // 2, (cross if kind % 2 else shifted)
        piece = jnp.where(lane < 32, src[16 * rb : 16 * rb + 8], src[16 * rb + 8 : 16 * rb + 16])
        value = jnp.where(spare, piece, packed)
        for i in range(4):
            for core in range(2):
                msg[pl.ds((2 * (4 * i + kind) + core) * 8, 8), :] = value


def sum_kernel(parts, msg):
    n = parts.shape[0] // 8
    s = parts[pl.ds(0, 8), :]
    for g in range(1, n):
        s = s + parts[pl.ds(8 * g, 8), :]
    for d in range(msg.shape[0] // 8):
        msg[pl.ds(8 * d, 8), :] = s


def basis_kernel(parts, share, msg, *, scale):
    n = parts.shape[0] // 8
    s = parts[pl.ds(0, 8), :]
    for g in range(1, n):
        s = s + parts[pl.ds(8 * g, 8), :]
    lane8 = iota((8, 128), 1) // 32
    rows = [all_blocks(jnp.where(lane8 == b, s, 0.0)) for b in range(4)]
    gram = jnp.concatenate(rows, axis=0)
    square = jnp.concatenate([gram] * 4, axis=0)
    flipped = square.T[:NP]
    row, lane = iota((NP, 128), 0), iota((NP, 128), 1)
    a = jnp.where((row < 16) & (lane % 32 >= 16), flipped, gram)
    a = jnp.where(lane < NP, a, jnp.where(lane - NP == row, 1.0, 0.0))
    for j in range(0, NP - 2, 2):
        f0 = jnp.broadcast_to(a[:, j : j + 1], a.shape)
        f1 = jnp.broadcast_to(a[:, j + 1 : j + 2], a.shape)
        r0, r1 = a[j : j + 1], a[j + 1 : j + 2]
        p, q, r = f0[j : j + 1], f0[j + 1 : j + 2], f1[j + 1 : j + 2]
        inv = 1.0 / (p * r - q * q)
        s0, s1 = (r * r0 - q * r1) * inv, (p * r1 - q * r0) * inv
        a = a - jnp.where(row > j + 1, f0 * s0 + f1 * s1, 0.0)
    above = pltpu.roll(a, 1, 0)
    left = lane == row - 1
    p = jnp.sum(jnp.where(left, above, 0.0), axis=1, keepdims=True)
    q = jnp.sum(jnp.where(left, a, 0.0), axis=1, keepdims=True)
    a = jnp.where(row % 2 == 1, a - (q / jnp.where(p > 0.0, p, 1.0)) * above, a)
    diag = jnp.sum(jnp.where(lane == row, a, 0.0), axis=1, keepdims=True)
    inverse = jnp.where(lane // 32 == 1, a * (scale / jnp.sqrt(diag)), 0.0)
    inverse = all_blocks(inverse)
    r = iota((NP, NP), 0)
    pick = (iota((NP, NP), 1) == 2 * (r % 16) + r // 16).astype(F32)
    rows = product(pick, inverse, ((1,), (0,)))[:, :NP]
    for x in range(8):
        out = product(rows, share[pl.ds(x * NP, NP), :], ((1,), (0,)))
        for j in range(2):
            msg[pl.ds(8 * j + x, 16, stride=24), :] = out[16 * j : 16 * j + 16]
    for d in range(16):
        msg[pl.ds(24 * d + 16, 8), :] = s


def finish_kernel(got, basis, core, *, factor):
    lane = iota((8, 128), 1)
    for j in range(2):
        for h in range(2):
            sources = [got[pl.ds(24 * (8 * h + d) + 8 * j, 8), :] for d in range(8)]
            for xt in range(2):
                for l in range(LV):
                    acc = jnp.zeros((8, 128), F32)
                    for d in range(8):
                        shift = (OWN * d - WIN * l - MARGIN - OWN * xt) % LANES
                        acc = jnp.where(lane // OWN == d, pltpu.roll(sources[d], shift, 1), acc)
                    basis[
                        pl.ds((j * LV + l) * RX + 8 * xt, 8), pl.ds(h * LANES, LANES)
                    ] = acc
    rows = []
    for rb in range(2):
        for half in range(2):
            first = 16 + 32 * half
            row = jnp.zeros((8, 128), F32)
            for cb in range(2):
                tile = got[pl.ds((3 * (2 * rb + cb) + 2) * 8, 8), :]
                moved = pltpu.roll(tile, (16 * cb - first) % 128, 1)
                row = jnp.where(lane // 16 == cb, moved, row)
            rows.append(row)
    core[...] = jnp.concatenate(rows, axis=0)[:, :NP] * factor


def shape(*dims):
    return jax.ShapeDtypeStruct(dims, F32)


def call(kernel, specs, outs, scratch=(), cost=None, grant=24 << 20):
    many = isinstance(outs, tuple)
    return pl.pallas_call(
        kernel,
        out_shape=outs,
        in_specs=specs,
        out_specs=(VM,) * len(outs) if many else VM,
        scratch_shapes=list(scratch),
        cost_estimate=cost,
        compiler_params=pltpu.CompilerParams(
            vmem_limit_bytes=grant
        ),
    )


def on_device(probes, wind, station_cell, obs_count, obs_weight):
    tiles, groups = lax.axis_size(SPACE), lax.axis_size("obs")
    layers, plane = lax.axis_size("z"), 2 * groups
    raw, patch, inner, outer = call(
        prepare_kernel,
        [pl.BlockSpec(memory_space=pltpu.HBM)] * 4 + [SM],
        (
            shape(KINDS * LV * RX, NY),
            shape(NP * RX, LANES),
            shape(MSG, LANES),
            shape(MSG, LANES),
        ),
        (
            pltpu.VMEM((NP * LV * RX, NY), F32),
            pltpu.VMEM((4 * LV * RX, NY), F32),
            pltpu.VMEM(station_cell.shape, jnp.int32),
            pltpu.VMEM(obs_weight.shape, F32),
            pltpu.SemaphoreType.DMA((7,)),
        ),
        grant=60 * 1024 * 1024,
    )(
        probes.reshape(NP * LV * RX, NY),
        wind.reshape(4 * LV * RX, NY),
        station_cell,
        obs_weight,
        obs_count,
    )
    inner = lax.ppermute(inner, SPACE, [(i, i ^ 1) for i in range(tiles)])
    across = [(i, i + 1) for i in range(1, tiles - 1, 2)]
    outer = lax.ppermute(outer, SPACE, across + [(b, a) for a, b in across])
    own = call(
        own_kernel,
        [VM],
        shape(groups * KINDS * RX, LANES),
        cost=pl.CostEstimate(flops=2000000, bytes_accessed=4000000, transcendentals=0),
    )(raw)
    msg = call(
        message_kernel,
        [VM] * 3,
        shape(groups * TALL, LANES),
        (pltpu.VMEM((KINDS * LV, 2, 8, LANES), F32),),
    )(own, inner, outer)
    got = lax.all_to_all(msg.reshape(groups, TALL, LANES), "obs", 0, 0, tiled=True)
    field = pltpu.VMEM((NP * ROWS, LANES), F32)
    padded = pltpu.VMEM((NP * ROWS + 2 * PAD, LANES), F32)
    share, msg = call(
        patch_kernel,
        [VM] * 4,
        (shape(8 * NP, LANES), shape(plane * 8, 128)),
        (
            padded,
            field,
            field,
            field,
            pltpu.VMEM((2 * 7 * LV * SLOT, LANES), F32),
            pltpu.VMEM((UNROLL * LV * SLOT, LANES), F32),
            pltpu.VMEM((UNROLL * LV * SLOT, LANES), F32),
            padded,
            padded,
            padded,
            pltpu.VMEM((NP * 8, LANES), F32),
            pltpu.VMEM((NP * 8, LANES), F32),
        ),
    )(got.reshape(groups * TALL, LANES), patch, inner, outer)
    got = lax.all_to_all(msg.reshape(plane, 8, 128), ("obs", "core"), 0, 0, tiled=True)
    msg = call(sum_kernel, [VM], shape(layers * 8, 128))(got.reshape(plane * 8, 128))
    got = lax.all_to_all(msg.reshape(layers, 8, 128), "z", 0, 0, tiled=True)
    scale = math.sqrt(LV * RX * tiles * NY)
    msg = call(
        lambda *refs: basis_kernel(*refs, scale=scale), [VM] * 2, shape(groups * 24, LANES)
    )(got.reshape(layers * 8, 128), share)
    got = lax.all_to_all(msg.reshape(groups, 24, LANES), "obs", 0, 0, tiled=True)
    factor = 1.0 / (groups * tiles * station_cell.shape[1])
    basis, core = call(
        lambda *refs: finish_kernel(*refs, factor=factor),
        [VM],
        (shape(2 * LV * RX, NY), shape(NP, NP)),
    )(got.reshape(groups * 24, LANES))
    return basis.reshape(2, LV, RX, NY), core


def solution(mesh):
    groups, tiles = mesh.shape["obs"], mesh.shape["space"]
    split = Mesh(mesh.devices.reshape(groups, tiles // 2, 2), ("obs", *SPACE))
    in_specs = (
        P(None, None, SPACE, None),
        P("obs", None, None, None, SPACE, None),
        P("obs", SPACE),
        P("obs", SPACE),
        P("obs", SPACE),
    )
    out_specs = (P("obs", None, SPACE, None), P())
    return jax.shard_map(
        on_device, mesh=split, in_specs=in_specs, out_specs=out_specs, check_vma=False
    )
```
